512 devices in a mesh: lag: 8 (over y), patch: 64 (over z, x, core).
Axes of the slice: x: 4, y: 8, z: 8, core: 2. Of those that a mesh axis runs over, the one named last changes fastest.
Arguments:
- incident: bfloat16 [4, 32768, 128], P(None, 'patch'), may hold values from -6 to 6
- pending: float32 [8, 32768, 128], P('lag', 'patch'), may hold values from -6 to 6
- self_inverse: float32 [256, 128, 128], P('patch'), may hold values from -0.5 to 0.5
- retarded: float32 [8, 64, 56, 128, 128], P('lag', 'patch'), may hold values from -0.1875 to 0.1875
- block_rows: int32 [8, 64, 56], P('lag', 'patch'), may hold values from -1 to 3, as said below
- block_sources: int32 [8, 64, 56], P('lag', 'patch'), may hold values from -1 to 255, as said below
- owner_map: int32 [256], replicated, may hold values from 0 to 255, as said below
Outputs:
- currents: bfloat16 [4, 32768, 128], P(None, 'patch')
- fields_ahead: float32 [8, 32768, 128], P('lag', 'patch')
The draws below stay inside these ranges and needn't reach their ends.
Inputs may be any that keep to these rules, and one draw needn't show every extreme that they name: `block_sources`: each device's list holds its live entries first and -1 after them; at most 56 live entries, a count that some device reaches in every draw; the live entries of one device name no (row, source) pair twice and, among them, at most one storage block of each patch owner. `block_rows`: -1 exactly where block_sources is -1. `owner_map`: A permutation of the 256 storage blocks; storage block q is owned by patch q // 4.
All inputs are finite; a program needn't handle non-finite values.
Results may differ from the reference program's by a relative error of at most 0.0055.
Values may be sent and summed in bfloat16 or wider, within the bound.
A program may use at most 64 MiB of HBM per device.

```python
import jax
import jax.numpy as jnp
from jax import lax

EXC = 128
BSIZE = 128
BLK_DEV = 4
BLOCKS_DEV = 56
STEPS = 4
LAGS = 8
PATCHES = 64
SRC = 256
UNKNOWNS = 32768


def layout_tables(key):
    base_key = jax.random.fold_in(key, 7)
    perm_key, count_key, full_key, order_key, row_key, local_key = jax.random.split(base_key, 6)
    owner_table = jax.random.permutation(perm_key, SRC).astype(jnp.int32)
    storage_source = jnp.argsort(owner_table).astype(jnp.int32)
    devices = LAGS * PATCHES
    lowest = BLOCKS_DEV - BLOCKS_DEV // 7
    counts = jax.random.randint(count_key, (devices,), lowest, BLOCKS_DEV + 1)
    full_device = jax.random.randint(full_key, (), 0, devices)
    counts = jnp.where(jnp.arange(devices) == full_device, BLOCKS_DEV, counts)
    order_keys = jax.random.split(order_key, devices)
    owner_orders = jax.vmap(lambda one_key: jax.random.permutation(one_key, PATCHES))(order_keys)
    entry = jnp.arange(BLOCKS_DEV)
    owner_patch = owner_orders[:, entry % PATCHES]
    base_rows = jax.random.randint(row_key, (devices, PATCHES), 0, BLK_DEV)
    start_row = jnp.take_along_axis(base_rows, owner_patch, axis=1)
    row_index = (start_row + (entry // PATCHES)[None, :]) % BLK_DEV
    local_pick = jax.random.randint(local_key, (devices, PATCHES), 0, BLK_DEV)
    chosen = jnp.take_along_axis(local_pick, owner_patch, axis=1)
    source_index = storage_source[owner_patch * BLK_DEV + chosen]
    is_live = entry[None, :] < counts[:, None]
    row_index = jnp.where(is_live, row_index, -1).reshape(LAGS, PATCHES, BLOCKS_DEV).astype(jnp.int32)
    source_index = jnp.where(is_live, source_index, -1).reshape(LAGS, PATCHES, BLOCKS_DEV).astype(jnp.int32)
    return (owner_table, row_index, source_index)


def draw_block_rows(key, part):
    return layout_tables(key)[1]


def draw_block_sources(key, part):
    return layout_tables(key)[2]


def draw_owner_map(key, part):
    return layout_tables(key)[0]


def shard_levels(own_key, dims, cuts, low, top_value):
    gain = 1.0
    for axis_at, shards_of in cuts:
        steps = jax.random.uniform(jax.random.fold_in(jax.random.fold_in(own_key, 6), axis_at), (shards_of,), jnp.float32, low / len(cuts), top_value / len(cuts))
        gain = gain * jnp.repeat(jnp.exp(steps), dims[axis_at] // shards_of).reshape((-1,) + (1,) * (len(dims) - 1 - axis_at))
    return gain


def noise(own_key, shape, scale, reach, cuts=(), held_as=jnp.bfloat16):
    result = jax.random.normal(own_key, shape, jnp.float32) * scale
    if len(cuts) > 0:
        result = shard_levels(own_key, shape, cuts, -0.22, 0.18) * result
    return jnp.clip(result, min=-reach, max=reach).astype(held_as)


def setup_inputs(seed: int = 0) -> dict:
    key_list = jax.random.split(jax.random.key(seed), 8)
    return {
        "incident": noise(key_list[0], (STEPS, UNKNOWNS, EXC), 1.0, 6.0, ((1, 64),)),
        "pending": noise(key_list[1], (LAGS, UNKNOWNS, EXC), 1.0, 6.0, ((0, 8), (1, 64)), jnp.float32),
        "self_inverse": noise(key_list[2], (SRC, BSIZE, BSIZE), BSIZE ** -0.5, 0.5, ((0, 64),), jnp.float32),
        "retarded": noise(key_list[3], (LAGS, PATCHES, BLOCKS_DEV, BSIZE, BSIZE), (BSIZE * 8) ** -0.5, 0.1875, ((0, 8), (1, 64)), jnp.float32),
        "block_rows": draw_block_rows(jax.random.fold_in(key_list[7], 71), 0),
        "block_sources": draw_block_sources(jax.random.fold_in(key_list[7], 71), 0),
        "owner_map": draw_owner_map(jax.random.fold_in(key_list[7], 71), 0),
    }


def reference(incident, pending, self_inverse, retarded, block_rows, block_sources, owner_map):
    fields = jnp.concatenate([pending, jnp.zeros((STEPS, UNKNOWNS, EXC), jnp.float32)], axis=0)
    row_choices = jnp.arange(BLK_DEV).astype(jnp.int32)
    currents = []
    for time_step in range(STEPS):
        excess = incident[time_step].astype(jnp.float32) - fields[time_step]
        solved = jnp.einsum("kab,kbe->kae", self_inverse, excess.reshape(SRC, BSIZE, EXC),
                            precision=lax.Precision.HIGHEST)
        current = solved.reshape(UNKNOWNS, EXC).astype(jnp.bfloat16)
        currents.append(current)
        source_blocks = current.reshape(SRC, BSIZE, EXC)

        def lag_term(operands):
            weights, row_index, source_index = operands
            is_live = (source_index >= 0).astype(jnp.float32)
            storage = owner_map[jnp.maximum(source_index, 0)]
            picked = source_blocks[storage].astype(jnp.float32) * is_live[:, :, None, None]
            product = jnp.einsum("pjab,pjbe->pjae", weights, picked, precision=lax.Precision.HIGHEST)
            row_select = (row_index[:, :, None] == row_choices[None, None, :]).astype(jnp.float32)
            summed = jnp.einsum("pjr,pjae->prae", row_select, product, precision=lax.Precision.HIGHEST)
            return summed.reshape(UNKNOWNS, EXC)

        terms = lax.map(lag_term, (retarded, block_rows, block_sources))
        fields = fields.at[time_step + 1:time_step + 1 + LAGS].add(terms)
    return jnp.stack(currents), fields[STEPS:STEPS + LAGS]
```

```python
import jax
import jax.numpy as jnp
from jax import lax
from jax.experimental import pallas as pl
from jax.experimental.pallas import tpu as pltpu
from jax.sharding import PartitionSpec as P

EXC = 128
B = 128
NB = 4
OWN = NB * B
STEPS = 4
LIST = 56
NX, NZ, NY = 4, 8, 8
MESH = pl.DeviceIdType.MESH

ORDER = (0, 1, 7, 2, 6, 3, 5, 4)
GROUPS = ((0, 1), (1, 3), (3, 5), (5, 7), (7, 8))
HALF = OWN // 2


def kernel(enc, inc, pend, sinv, want, zmat, cur_out, ahead_out,
           zf, w, items, pick, sbuf, rbuf, part, shift, acc, wanted, onehot,
           load_sem, bc_r, z_r, x_r, r_r, sh_r, q_r, bc_s, z_s, x_s, r_s, sh_s, q_s):
    y = lax.axis_index("lag")
    p = lax.axis_index("patch")
    c = lax.rem(p, 2)
    x = lax.rem(lax.div(p, 2), NX)
    z = lax.div(p, 2 * NX)

    def at(dx=0, dz=0, core=None):
        core = c if core is None else core
        return lax.rem(z + dz + NZ, NZ) * (2 * NX) + lax.rem(x + dx, NX) * 2 + core

    def dev(patch, lag=None):
        return {"lag": y if lag is None else lag, "patch": patch}

    up, down = lax.rem(y + 1, NY), lax.rem(y + NY - 1, NY)
    partner = 1 - c
    peers = [dev(at(dz=1)), dev(at(dz=-1)), dev(at(core=partner)), dev(p, up), dev(p, down)]
    peers += [dev(at(dx=dx, core=k)) for dx in (1, 2, 3) for k in (0, 1)]

    load = pltpu.make_async_copy(zmat.at[0, 0], zf, load_sem)
    load.start()

    barrier = pltpu.get_barrier_semaphore()
    for peer in peers:
        pl.semaphore_signal(barrier, inc=1, device_id=peer, device_id_type=MESH)
    pl.semaphore_wait(barrier, len(peers))

    def remote(src, dst, ssem, rsem, where):
        return pltpu.make_async_remote_copy(
            src_ref=src, dst_ref=dst, send_sem=ssem, recv_sem=rsem,
            device_id=where, device_id_type=MESH)

    def asks():
        out = [remote(want.at[1 - c], wanted.at[c], q_s.at[0], q_r.at[c], dev(at(core=partner)))]
        for dx in (1, 2, 3):
            for k in (0, 1):
                t, back = dx * 2 + k, (NX - dx) * 2
                out.append(remote(want.at[t], wanted.at[back + c], q_s.at[t - 1], q_r.at[back + c],
                                  dev(at(dx=dx, core=k))))
        return out

    for copy in asks():
        copy.start()

    part[0] = pend[0]

    def step(n, carry):
        def bcast(k, lag, sem):
            rows = pl.ds(k * HALF, HALF)
            return remote(items.at[n, 0, rows], items.at[n, 0, rows], bc_s.at[sem, k], bc_r.at[n, k],
                          dev(p, lag))

        def ring(d_from, d_to, k, dz):
            rows = pl.ds(k * HALF, HALF)
            return remote(items.at[n, d_from, rows], items.at[n, d_to, rows], z_s.at[d_to, k],
                          z_r.at[n, d_to, k], dev(at(dz=dz)))

        def sends(g):
            p0, p1 = GROUPS[g]
            span = pl.ds(p0, p1 - p0)
            out = [remote(sbuf.at[0, span], pick.at[n, span, pl.ds(pl.multiple_of(c * B, B), B)],
                          x_s.at[g, 0], x_r.at[n, g, c], dev(at(core=partner)))]
            for dx in (1, 3):
                for k in (0, 1):
                    t, back = dx * 2 + k, (NX - dx) * 2 + c
                    out.append(remote(
                        sbuf.at[t, span], pick.at[n, span, pl.ds(pl.multiple_of(back * B, B), B)],
                        x_s.at[g, t - 1], x_r.at[n, g, back], dev(at(dx=dx, core=k))))
            for k, dx in ((0, 1), (1, 3)):
                out.append(remote(sbuf.at[4 + k, span], rbuf.at[n, k, span], x_s.at[g, 3 + k],
                                  r_r.at[n, g, k], dev(at(dx=dx))))
            return out

        def relays(g):
            p0, p1 = GROUPS[g]
            span = pl.ds(p0, p1 - p0)
            rows = pl.ds(pl.multiple_of((4 + c) * B, B), B)
            return [remote(rbuf.at[n, k, span], pick.at[n, span, rows], r_s.at[g, k],
                           x_r.at[n, g, 4 + c], dev(at(dx=dx, core=k))) for k, dx in ((0, 1), (1, 3))]

        def select(pos):
            whole = items[n, ORDER[pos]].reshape(NB, B // 16, 16, EXC)

            def choose(t):
                total = whole[0] * onehot[t, pos * NB][None]
                for k in range(1, NB):
                    total = total + whole[k] * onehot[t, pos * NB + k][None]
                return total.reshape(B, EXC)

            pick[n, pos, pl.ds(pl.multiple_of(c * B, B), B), :] = choose(c)
            sbuf[0, pos] = choose(partner)
            for t in range(2, 8):
                sbuf[t, pos] = choose(t)

        def pass_on(g):
            for pos in range(*GROUPS[g]):
                select(pos)
            for copy in sends(g):
                copy.start()

        def relay(g):
            p0, p1 = GROUPS[g]
            span = pl.ds(p0, p1 - p0)
            for k, copy in enumerate(relays(g)):
                remote(rbuf.at[n, k, span], rbuf.at[n, k, span], r_s.at[g, k], r_r.at[n, g, k],
                       dev(p, up)).wait_recv()
                copy.start()

        def apply(g):
            p0, p1 = GROUPS[g]
            span = pl.ds(p0, p1 - p0)
            for s in range(8):
                block = pick.at[n, span, pl.ds(s * B, B)]
                wait = remote(block, block, x_s.at[g, 0], x_r.at[n, g, s], dev(p, up)).wait_recv
                if s < 2:
                    pl.when(c != s)(wait)
                else:
                    wait()
            for pos in range(p0, p1):
                term = jnp.dot(w[pos], pick[n, pos], preferred_element_type=jnp.float32)
                if pos == 0:
                    acc[...] = term
                else:
                    acc[...] += term

        first = n == 0

        @pl.when(y == 0)
        def _():
            for k in range(NB):
                rows = slice(k * B, (k + 1) * B)
                excess = inc[n, rows].astype(jnp.float32) - part[n, rows]
                solved = jnp.dot(sinv[k], excess, precision=lax.Precision.HIGHEST,
                                 preferred_element_type=jnp.float32)
                items[n, 0, rows] = solved.astype(jnp.bfloat16)

        goes_up = [y <= 3, y <= 2]
        goes_down = [(y == 0) | (y >= 6), (y == 0) | (y >= 5)]
        for k in range(2):
            pl.when(y != 0)(bcast(k, up, 0).wait_recv)
            pl.when(goes_up[k])(bcast(k, up, 0).start)
            pl.when(goes_down[k])(bcast(k, down, 1).start)
            ring(0, 1, k, 1).start()
            ring(0, 7, k, -1).start()

        @pl.when(first)
        def _():
            for t in range(8):
                if t < 2:
                    pl.when(c != t)(remote(wanted.at[t], wanted.at[t], q_s.at[0], q_r.at[t], dev(p, up)).wait_recv)
                else:
                    remote(wanted.at[t], wanted.at[t], q_s.at[0], q_r.at[t], dev(p, up)).wait_recv()
            wanted[c] = want[c]

            def spread(t, carry):
                for r in range(NB * NZ):
                    onehot[t, r] = jnp.broadcast_to(wanted[t, pl.ds(r, 1), :], (16, EXC)).astype(jnp.bfloat16)
                return carry

            lax.fori_loop(0, 8, spread, 0)

        pass_on(0)
        cur_out[n] = items[n, 0]
        move = remote(part.at[n], shift.at[n], sh_s, sh_r.at[n], dev(p, down))
        pl.when(y != 0)(move.start)

        for k in range(2):
            ring(0, 1, k, 1).wait_recv()
            ring(1, 2, k, 1).start()
            ring(0, 7, k, -1).wait_recv()
            ring(7, 6, k, -1).start()
        pass_on(1)
        relay(0)
        for k in range(2):
            ring(1, 2, k, 1).wait_recv()
            ring(2, 3, k, 1).start()
            ring(7, 6, k, -1).wait_recv()
            ring(6, 5, k, -1).start()
        pass_on(2)
        relay(1)
        for k in range(2):
            ring(2, 3, k, 1).wait_recv()
            ring(6, 5, k, -1).wait_recv()
            if k == 0:
                ring(3, 4, 0, 1).start()
            else:
                ring(5, 4, 1, -1).start()
        pass_on(3)
        relay(2)
        ring(3, 4, 0, 1).wait_recv()
        ring(5, 4, 1, -1).wait_recv()
        pass_on(4)

        @pl.when(first)
        def _():
            pltpu.make_async_copy(zmat.at[0, 0], zf, load_sem).wait()

            def place(s, carry):
                code = enc[s]
                row = jnp.where(code < 0, -1, (code >> 2) & 3)
                block = zf[jnp.maximum(code, 0) >> 4].astype(jnp.bfloat16)
                pos, col = lax.div(s, 8), lax.rem(s, 8)
                for r in range(NB):
                    keep = jnp.where(row == r, 1.0, 0.0).astype(jnp.bfloat16)
                    w[pos, pl.ds(r * B, B), pl.ds(pl.multiple_of(col * B, B), B)] = block * keep
                return carry

            lax.fori_loop(0, 64, place, 0)

        relay(3)
        apply(0)
        relay(4)
        for g in range(1, 5):
            apply(g)

        pl.when(y != NY - 1)(move.wait_recv)

        @pl.when(y != NY - 1)
        def _():
            part[n + 1] = acc[...] + shift[n]

        @pl.when(y == NY - 1)
        def _():
            part[n + 1] = acc[...]

        for k in range(2):
            pl.when(goes_up[k])(bcast(k, up, 0).wait_send)
            pl.when(goes_down[k])(bcast(k, down, 1).wait_send)
            for d_from, d_to, dz in ((0, 1, 1), (1, 2, 1), (2, 3, 1), (0, 7, -1), (7, 6, -1), (6, 5, -1)):
                ring(d_from, d_to, k, dz).wait_send()
        ring(3, 4, 0, 1).wait_send()
        ring(5, 4, 1, -1).wait_send()
        for g in range(5):
            for copy in sends(g) + relays(g):
                copy.wait_send()
        pl.when(y != 0)(move.wait_send)
        return carry

    lax.fori_loop(0, STEPS, step, 0)
    for copy in asks():
        copy.wait_send()
    ahead_out[0] = part[STEPS]


def body(incident, pending, self_inverse, retarded, block_rows, block_sources, owner_map):
    p = lax.axis_index("patch")
    x, z = (p // 2) % NX, p // (2 * NX)
    row = block_rows[0, 0]
    source = block_sources[0, 0]
    live = source >= 0
    storage = owner_map[jnp.maximum(source, 0)]
    owner, local = storage // NB, storage % NB
    d = (z - owner // (2 * NX)) % NZ
    pos = jnp.where(d == 0, 0, jnp.where(d <= 3, 2 * d - 1, jnp.where(d == 4, 7, 2 * (NZ - d))))
    column = ((owner // 2) % NX - x) % NX * 2 + owner % 2
    slot = pos * 8 + column
    code = jnp.arange(LIST, dtype=jnp.int32) * 16 + row * 4 + local
    hit = (slot[None, :] == jnp.arange(64)[:, None]) & live[None, :]
    enc = jnp.max(jnp.where(hit, code[None, :], -1), axis=1).astype(jnp.int32)
    picked = jnp.maximum(enc, 0) % NB
    wants = (picked.reshape(NZ, 8).T[:, :, None] == jnp.arange(NB)).astype(jnp.float32)
    want = jnp.broadcast_to(wants.reshape(8, NZ * NB)[:, :, None], (8, NZ * NB, EXC))

    vmem = pl.BlockSpec(memory_space=pltpu.VMEM)
    dma = pltpu.SemaphoreType.DMA
    return pl.pallas_call(
        kernel,
        out_shape=(jax.ShapeDtypeStruct((STEPS, OWN, EXC), jnp.bfloat16),
                   jax.ShapeDtypeStruct((1, OWN, EXC), jnp.float32)),
        in_specs=[pl.BlockSpec(memory_space=pltpu.SMEM), vmem, vmem, vmem, vmem,
                  pl.BlockSpec(memory_space=pl.ANY)],
        out_specs=(vmem, vmem),
        scratch_shapes=[
            pltpu.VMEM((LIST, B, B), jnp.float32),
            pltpu.VMEM((NZ, OWN, 8 * B), jnp.bfloat16),
            pltpu.VMEM((STEPS, NZ, OWN, EXC), jnp.bfloat16),
            pltpu.VMEM((STEPS, NZ, 8 * B, EXC), jnp.bfloat16),
            pltpu.VMEM((8, NZ, B, EXC), jnp.bfloat16),
            pltpu.VMEM((STEPS, 2, NZ, B, EXC), jnp.bfloat16),
            pltpu.VMEM((STEPS + 1, OWN, EXC), jnp.float32),
            pltpu.VMEM((STEPS, OWN, EXC), jnp.float32),
            pltpu.VMEM((OWN, EXC), jnp.float32),
            pltpu.VMEM((8, NZ * NB, EXC), jnp.float32),
            pltpu.VMEM((8, NZ * NB, 16, EXC), jnp.bfloat16),
            dma, dma((STEPS, 2)), dma((STEPS, NZ, 2)), dma((STEPS, 5, 8)), dma((STEPS, 5, 2)),
            dma((STEPS,)), dma((8,)),
            dma((2, 2)), dma((NZ, 2)), dma((5, 7)), dma((5, 2)), dma, dma((8,)),
        ],
        compiler_params=pltpu.CompilerParams(collective_id=0, has_side_effects=True,
                                             vmem_limit_bytes=60 * 1024 * 1024),
    )(enc, incident, pending, self_inverse, want, retarded)


def solution(mesh):
    in_specs = (
        P(None, "patch", None),
        P("lag", "patch", None),
        P("patch", None, None),
        P("lag", "patch", None, None, None),
        P("lag", "patch", None),
        P("lag", "patch", None),
        P(),
    )
    out_specs = (P(None, "patch", None), P("lag", "patch", None))
    return jax.shard_map(body, mesh=mesh, in_specs=in_specs, out_specs=out_specs, check_vma=False)
```

```python
import jax
import jax.numpy as jnp
from jax import lax
from jax.experimental import pallas as pl
from jax.experimental.pallas import tpu as pltpu
from jax.sharding import PartitionSpec as P

EXC = 128
B = 128
NB = 4
OWN = NB * B
STEPS = 4
LIST = 56
SRC = 256
NX, NZ, NY = 4, 8, 8
MESH = pl.DeviceIdType.MESH

ORDER = (0, 1, 7, 2, 6, 3, 5, 4)
GROUPS = ((0, 1), (1, 3), (3, 5), (5, 7), (7, 8))
MAIN, SLAB = 96, 32


def kernel(enc, inc, pend, sinv, zmat, cur_out, ahead_out,
           zf, w, items, slabs, pick, sbuf, pbuf, qbuf, rbuf, part, shift, acc, want, wanted, wanted2, onehot,
           load_sem, bc_r, z_r, s_r, x_r, r_r, p_r, sh_r, q_r,
           bc_s, z_s, s_s, x_s, r_s, p_s, sh_s, q_s):
    y = lax.axis_index("lag")
    p = lax.axis_index("patch")
    c = lax.rem(p, 2)
    x = lax.rem(lax.div(p, 2), NX)
    z = lax.div(p, 2 * NX)

    def at(dx=0, dz=0, core=None):
        core = c if core is None else core
        return lax.rem(z + dz + NZ, NZ) * (2 * NX) + lax.rem(x + dx, NX) * 2 + core

    def dev(patch, lag=None):
        return {"lag": y if lag is None else lag, "patch": patch}

    up, down = lax.rem(y + 1, NY), lax.rem(y + NY - 1, NY)
    partner = 1 - c
    mate = dev(at(core=partner))
    peers = [dev(at(dz=1)), dev(at(dz=-1)), mate, dev(p, up), dev(p, down)]
    peers += [dev(at(dx=dx, core=k)) for dx in (1, 2, 3) for k in (0, 1)]

    load = pltpu.make_async_copy(zmat.at[0, 0], zf, load_sem)
    load.start()

    barrier = pltpu.get_barrier_semaphore()
    for peer in peers:
        pl.semaphore_signal(barrier, inc=1, device_id=peer, device_id_type=MESH)

    def ask(s, carry):
        pos, t = lax.div(s, 8), lax.rem(s, 8)
        local = jnp.maximum(enc[s], 0) & 3
        for k in range(NB):
            want[t, pl.ds(pos * NB + k, 1), :] = jnp.full((1, EXC), jnp.where(local == k, 1.0, 0.0), jnp.float32)
        return carry

    lax.fori_loop(0, 64, ask, 0)
    part[0] = pend[0]
    pl.semaphore_wait(barrier, len(peers))

    def remote(src, dst, ssem, rsem, where):
        return pltpu.make_async_remote_copy(
            src_ref=src, dst_ref=dst, send_sem=ssem, recv_sem=rsem,
            device_id=where, device_id_type=MESH)

    def arrives(ref, rsem):
        return remote(ref, ref, sh_s, rsem, mate).wait_recv

    def asks():
        out = [remote(want.at[partner], wanted.at[c], q_s.at[0], q_r.at[c], mate)]
        for dx in (1, 2, 3):
            out.append(remote(want.at[dx * 2 + partner], wanted2.at[dx - 1], q_s.at[6 + dx], q_r.at[7 + dx], mate))
            for k in (0, 1):
                t, back = dx * 2 + k, (NX - dx) * 2
                out.append(remote(want.at[t], wanted.at[back + c], q_s.at[t - 1], q_r.at[back + c],
                                  dev(at(dx=dx, core=k))))
        return out

    for copy in asks():
        copy.start()

    def step(n, carry):
        def mine(row):
            return pl.ds(pl.multiple_of(row * B, B), B)

        def bcast(i, lag, sem):
            piece = items.at[n, 0, i // 2, pl.ds((i % 2) * (B // 2), B // 2)]
            return remote(piece, piece, bc_s.at[sem, i], bc_r.at[n, i], dev(p, lag))

        def ring(d_from, d_to, k, dz):
            half = pl.ds(2 * k, 2)
            return remote(items.at[n, d_from, half], items.at[n, d_to, half], z_s.at[d_to, k],
                          z_r.at[n, d_to, k], dev(at(dz=dz)))

        def slab_start():
            return [remote(items.at[n, 0, :, pl.ds(MAIN, SLAB)], slabs.at[n, 0, NX - dx - 1], s_s.at[0, dx - 1],
                           s_r.at[n, 0, NX - dx - 1], dev(at(dx=dx))) for dx in (2, 1, 3)]

        def slab_ring(d_from, d_to, k, dz):
            half = pl.ds(2 * k, 2)
            return remote(slabs.at[n, d_from, :, half], slabs.at[n, d_to, :, half], s_s.at[d_to, k],
                          s_r.at[n, d_to, k], dev(at(dz=dz)))

        def span_of(g):
            p0, p1 = GROUPS[g]
            return pl.ds(p0, p1 - p0)

        def sends(g):
            span = span_of(g)
            out = []
            for k, dx in ((0, 1), (1, 3)):
                out.append(remote(sbuf.at[2 + k, span], rbuf.at[n, k, span], x_s.at[g, 3 + k],
                                  r_r.at[n, g, k], dev(at(dx=dx))))
            for dx in (1, 3):
                for k in (0, 1):
                    t, back = dx * 2 + k, (NX - dx) * 2 + c
                    out.append(remote(
                        sbuf.at[t - 2, span], pick.at[n, span, pl.ds(pl.multiple_of(back * B, B), MAIN)],
                        x_s.at[g, t - 1], x_r.at[n, g, back], dev(at(dx=dx, core=k))))
            out.append(remote(pbuf.at[span], pick.at[n, span, mine(c)], x_s.at[g, 0], x_r.at[n, g, c], mate))
            return out

        def slab_sends(g):
            span = span_of(g)
            return [remote(qbuf.at[dx - 1, span],
                           pick.at[n, span, pl.ds(pl.multiple_of((dx * 2 + c) * B + MAIN, SLAB), SLAB)],
                           p_s.at[g, dx - 1], p_r.at[n, g, dx - 1], mate) for dx in (1, 2, 3)]

        def relays(g):
            span = span_of(g)
            rows = pl.ds(pl.multiple_of((4 + c) * B, B), MAIN)
            return [remote(rbuf.at[n, k, span], pick.at[n, span, rows], r_s.at[g, k],
                           x_r.at[n, g, 4 + c], dev(at(dx=dx, core=k))) for k, dx in ((0, 1), (1, 3))]

        def choose(blocks, table, pos, rows):
            total = None
            for k in range(NB):
                term = blocks[k].reshape(rows // 16, 16, EXC) * onehot[table, pos * NB + k][None]
                total = term if total is None else total + term
            return total.reshape(rows, EXC)

        def pass_on(g):
            for pos in range(*GROUPS[g]):
                whole = [items[n, ORDER[pos], k] for k in range(NB)]
                head = [block[:MAIN] for block in whole]
                for t in (4, 5, 2, 3, 6, 7):
                    sbuf[t - 2, pos] = choose(head, t, pos, MAIN)
                pbuf[pos] = choose(whole, partner, pos, B)
                pick[n, pos, mine(c), :] = choose(whole, c, pos, B)
            for copy in sends(g):
                copy.start()

        def slab_pass(g):
            for pos in range(*GROUPS[g]):
                for dx in (1, 2, 3):
                    blocks = [slabs[n, ORDER[pos], dx - 1, k] for k in range(NB)]
                    qbuf[dx - 1, pos] = choose(blocks, 11 + dx - 1, pos, SLAB)
                    rows = pl.ds(pl.multiple_of((dx * 2 + c) * B + MAIN, SLAB), SLAB)
                    pick[n, pos, rows, :] = choose(blocks, 8 + dx - 1, pos, SLAB)
            for copy in slab_sends(g):
                copy.start()

        def relay(g):
            for k, copy in enumerate(relays(g)):
                arrives(rbuf.at[n, k, span_of(g)], r_r.at[n, g, k])()
                copy.start()

        def apply(g):
            span = span_of(g)
            for s in range(8):
                if s < 2:
                    pl.when(c != s)(arrives(pick.at[n, span, pl.ds(s * B, B)], x_r.at[n, g, s]))
                else:
                    arrives(pick.at[n, span, pl.ds(s * B, MAIN)], x_r.at[n, g, s])()
            for dx in (1, 2, 3):
                rows = pl.ds(pl.multiple_of((dx * 2 + partner) * B + MAIN, SLAB), SLAB)
                arrives(pick.at[n, span, rows], p_r.at[n, g, dx - 1])()
            for pos in range(*GROUPS[g]):
                term = jnp.dot(w[pos], pick[n, pos], preferred_element_type=jnp.float32)
                if pos == 0:
                    acc[...] = term
                else:
                    acc[...] += term

        first = n == 0

        @pl.when(y == 0)
        def _():
            for k in range(NB):
                rows = slice(k * B, (k + 1) * B)
                excess = inc[n, rows].astype(jnp.float32) - part[n, rows]
                solved = jnp.dot(sinv[k], excess, precision=lax.Precision.HIGHEST,
                                 preferred_element_type=jnp.float32)
                items[n, 0, k] = solved.astype(jnp.bfloat16)

        goes_up = [y <= 3, y <= 2]
        goes_down = [(y == 0) | (y >= 6), (y == 0) | (y >= 5)]
        for i in range(8):
            piece = items.at[n, 0, i // 2, pl.ds((i % 2) * (B // 2), B // 2)]
            pl.when(y != 0)(arrives(piece, bc_r.at[n, i]))
            pl.when(goes_up[i // 4])(bcast(i, up, 0).start)
            pl.when(goes_down[i // 4])(bcast(i, down, 1).start)
            if i % 4 == 3:
                ring(0, 1, i // 4, 1).start()
                ring(0, 7, i // 4, -1).start()
        for copy in slab_start():
            copy.start()

        @pl.when(first)
        def _():
            for t in range(8):
                if t < 2:
                    pl.when(c != t)(arrives(wanted.at[t], q_r.at[t]))
                else:
                    arrives(wanted.at[t], q_r.at[t])()
            wanted[c] = want[c]
            for dx in (1, 2, 3):
                arrives(wanted2.at[dx - 1], q_r.at[7 + dx])()

            def line(rows):
                return jnp.broadcast_to(rows, (16, EXC)).astype(jnp.bfloat16)

            def spread(t, carry):
                for r in range(NB * NZ):
                    onehot[t, r] = line(wanted[t, pl.ds(r, 1), :])
                return carry

            def spread_slabs(i, carry):
                for r in range(NB * NZ):
                    onehot[8 + i, r] = line(want[i * 2 + 2 + c, pl.ds(r, 1), :])
                    onehot[11 + i, r] = line(wanted2[i, pl.ds(r, 1), :])
                return carry

            lax.fori_loop(0, 8, spread, 0)
            lax.fori_loop(0, 3, spread_slabs, 0)

        pass_on(0)
        cur_out[n] = items[n, 0].reshape(OWN, EXC)
        move = remote(part.at[n], shift.at[n], sh_s, sh_r.at[n], dev(p, down))
        pl.when(y != 0)(move.start)

        def hop(make, a, b, arrive):
            for k in range(2):
                make(a[0] - 1, a[0], k, 1).wait_recv()
                if arrive == 3:
                    if k == 0:
                        make(a[0], 4, 0, 1).start()
                else:
                    make(a[0], a[0] + 1, k, 1).start()
                make(b[0], b[0], k, -1).wait_recv()
                if arrive == 3:
                    if k == 1:
                        make(b[0], 4, 1, -1).start()
                else:
                    make(b[0], b[0] - 1, k, -1).start()

        hop(ring, (1,), (7,), 1)
        for i in range(3):
            arrives(slabs.at[n, 0, i], s_r.at[n, 0, i])()
        for k in range(2):
            slab_ring(0, 1, k, 1).start()
            slab_ring(0, 7, k, -1).start()
        pass_on(1)
        hop(ring, (2,), (6,), 2)
        relay(0)
        hop(slab_ring, (1,), (7,), 1)
        pass_on(2)
        slab_pass(0)
        hop(ring, (3,), (5,), 3)
        relay(1)
        pass_on(3)
        hop(slab_ring, (2,), (6,), 2)
        slab_pass(1)

        @pl.when(first)
        def _():
            pltpu.make_async_copy(zmat.at[0, 0], zf, load_sem).wait()

            def place(s, carry):
                code = enc[s]
                row = jnp.where(code < 0, -1, (code >> 2) & 3)
                block = zf[jnp.maximum(code, 0) >> 4].astype(jnp.bfloat16)
                pos, col = lax.div(s, 8), lax.rem(s, 8)
                for r in range(NB):
                    keep = jnp.where(row == r, 1.0, 0.0).astype(jnp.bfloat16)
                    w[pos, pl.ds(r * B, B), pl.ds(pl.multiple_of(col * B, B), B)] = block * keep
                return carry

            lax.fori_loop(0, 64, place, 0)

        relay(2)
        ring(3, 4, 0, 1).wait_recv()
        ring(5, 4, 1, -1).wait_recv()
        pass_on(4)
        apply(0)
        hop(slab_ring, (3,), (5,), 3)
        slab_pass(2)
        relay(3)
        apply(1)
        slab_pass(3)
        relay(4)
        apply(2)
        slab_ring(3, 4, 0, 1).wait_recv()
        slab_ring(5, 4, 1, -1).wait_recv()
        slab_pass(4)
        apply(3)
        apply(4)

        pl.when(y != NY - 1)(move.wait_recv)

        @pl.when(y != NY - 1)
        def _():
            part[n + 1] = acc[...] + shift[n]

        @pl.when(y == NY - 1)
        def _():
            part[n + 1] = acc[...]

        for i in range(8):
            pl.when(goes_up[i // 4])(bcast(i, up, 0).wait_send)
            pl.when(goes_down[i // 4])(bcast(i, down, 1).wait_send)
        for make in (ring, slab_ring):
            for k in range(2):
                for d_from, d_to, dz in ((0, 1, 1), (1, 2, 1), (2, 3, 1), (0, 7, -1), (7, 6, -1), (6, 5, -1)):
                    make(d_from, d_to, k, dz).wait_send()
            make(3, 4, 0, 1).wait_send()
            make(5, 4, 1, -1).wait_send()
        for copy in slab_start():
            copy.wait_send()
        for g in range(5):
            for copy in sends(g) + relays(g) + slab_sends(g):
                copy.wait_send()
        pl.when(y != 0)(move.wait_send)
        return carry

    lax.fori_loop(0, STEPS, step, 0)
    for copy in asks():
        copy.wait_send()
    ahead_out[0] = part[STEPS]


def body(incident, pending, self_inverse, retarded, block_rows, block_sources, owner_map):
    p = lax.axis_index("patch")
    x, z = (p // 2) % NX, p // (2 * NX)
    row = block_rows[0, 0]
    source = block_sources[0, 0]
    live = source >= 0
    storage = jnp.sum(jnp.where(source[:, None] == jnp.arange(SRC)[None, :], owner_map[None, :], 0), axis=1)
    owner, local = storage // NB, storage % NB
    d = (z - owner // (2 * NX)) % NZ
    pos = jnp.where(d == 0, 0, jnp.where(d <= 3, 2 * d - 1, jnp.where(d == 4, 7, 2 * (NZ - d))))
    column = ((owner // 2) % NX - x) % NX * 2 + owner % 2
    slot = pos * 8 + column
    code = jnp.arange(LIST, dtype=jnp.int32) * 16 + row * 4 + local
    hit = (slot[None, :] == jnp.arange(64)[:, None]) & live[None, :]
    enc = jnp.max(jnp.where(hit, code[None, :], -1), axis=1).astype(jnp.int32)
    vmem = pl.BlockSpec(memory_space=pltpu.VMEM)
    dma = pltpu.SemaphoreType.DMA
    return pl.pallas_call(
        kernel,
        out_shape=(jax.ShapeDtypeStruct((STEPS, OWN, EXC), jnp.bfloat16),
                   jax.ShapeDtypeStruct((1, OWN, EXC), jnp.float32)),
        in_specs=[pl.BlockSpec(memory_space=pltpu.SMEM), vmem, vmem, vmem,
                  pl.BlockSpec(memory_space=pl.ANY)],
        out_specs=(vmem, vmem),
        scratch_shapes=[
            pltpu.VMEM((LIST, B, B), jnp.float32),
            pltpu.VMEM((NZ, OWN, 8 * B), jnp.bfloat16),
            pltpu.VMEM((STEPS, NZ, NB, B, EXC), jnp.bfloat16),
            pltpu.VMEM((STEPS, NZ, NX - 1, NB, SLAB, EXC), jnp.bfloat16),
            pltpu.VMEM((STEPS, NZ, 8 * B, EXC), jnp.bfloat16),
            pltpu.VMEM((6, NZ, MAIN, EXC), jnp.bfloat16),
            pltpu.VMEM((NZ, B, EXC), jnp.bfloat16),
            pltpu.VMEM((NX - 1, NZ, SLAB, EXC), jnp.bfloat16),
            pltpu.VMEM((STEPS, 2, NZ, MAIN, EXC), jnp.bfloat16),
            pltpu.VMEM((STEPS + 1, OWN, EXC), jnp.float32),
            pltpu.VMEM((STEPS, OWN, EXC), jnp.float32),
            pltpu.VMEM((OWN, EXC), jnp.float32),
            pltpu.VMEM((8, NZ * NB, EXC), jnp.float32),
            pltpu.VMEM((8, NZ * NB, EXC), jnp.float32),
            pltpu.VMEM((NX - 1, NZ * NB, EXC), jnp.float32),
            pltpu.VMEM((14, NZ * NB, 16, EXC), jnp.bfloat16),
            dma, dma((STEPS, 8)), dma((STEPS, NZ, 2)), dma((STEPS, NZ, 3)), dma((STEPS, 5, 8)), dma((STEPS, 5, 2)),
            dma((STEPS, 5, 3)), dma((STEPS,)), dma((11,)),
            dma((2, 8)), dma((NZ, 2)), dma((NZ, 3)), dma((5, 7)), dma((5, 2)), dma((5, 3)), dma, dma((10,)),
        ],
        compiler_params=pltpu.CompilerParams(collective_id=0, has_side_effects=True,
                                             vmem_limit_bytes=48 * 1024 * 1024),
    )(enc, incident, pending, self_inverse, retarded)


def solution(mesh):
    in_specs = (
        P(None, "patch", None),
        P("lag", "patch", None),
        P("patch", None, None),
        P("lag", "patch", None, None, None),
        P("lag", "patch", None),
        P("lag", "patch", None),
        P(),
    )
    out_specs = (P(None, "patch", None), P("lag", "patch", None))
    return jax.shard_map(body, mesh=mesh, in_specs=in_specs, out_specs=out_specs, check_vma=False)
```

```python
import jax
import jax.numpy as jnp
from jax import lax
from jax.experimental import pallas as pl
from jax.experimental.pallas import tpu as pltpu
from jax.sharding import PartitionSpec as P

EXC = 128
B = 128
NB = 4
OWN = NB * B
STEPS = 4
LIST = 56
SRC = 256
NX, NZ, NY = 4, 8, 8
MESH = pl.DeviceIdType.MESH

ORDER = (0, 1, 7, 2, 6, 3, 5, 4)
GROUPS = ((0, 1), (1, 3), (3, 5), (5, 7), (7, 8))
MAIN, SLAB = 96, 32


def kernel(enc, inc_hbm, pend, sinv_hbm, zmat, cur_out, ahead_out,
           inc, sinv, zf, w, items, slabs, pick, sbuf, pbuf, qbuf, rbuf, part, shift, acc, want, wanted, wanted2, onehot,
           load_sem, bc_r, z_r, s_r, x_r, r_r, p_r, sh_r, q_r,
           bc_s, z_s, s_s, x_s, r_s, p_s, sh_s, q_s):
    y = lax.axis_index("lag")
    p = lax.axis_index("patch")
    c = lax.rem(p, 2)
    x = lax.rem(lax.div(p, 2), NX)
    z = lax.div(p, 2 * NX)

    def at(dx=0, dz=0, core=None):
        core = c if core is None else core
        return lax.rem(z + dz + NZ, NZ) * (2 * NX) + lax.rem(x + dx, NX) * 2 + core

    def dev(patch, lag=None):
        return {"lag": y if lag is None else lag, "patch": patch}

    up, down = lax.rem(y + 1, NY), lax.rem(y + NY - 1, NY)
    partner = 1 - c
    mate = dev(at(core=partner))
    peers = [dev(at(dz=1)), dev(at(dz=-1)), mate, dev(p, up), dev(p, down)]
    peers += [dev(at(dx=dx, core=k)) for dx in (1, 2, 3) for k in (0, 1)]

    loads = [pltpu.make_async_copy(pend.at[0], part.at[0], load_sem.at[0]),
             pltpu.make_async_copy(inc_hbm, inc, load_sem.at[1]),
             pltpu.make_async_copy(sinv_hbm, sinv, load_sem.at[2]),
             pltpu.make_async_copy(zmat.at[0, 0], zf, load_sem.at[3])]

    barrier = pltpu.get_barrier_semaphore()
    for peer in peers:
        pl.semaphore_signal(barrier, inc=1, device_id=peer, device_id_type=MESH)
    for load in loads:
        load.start()

    def ask(s, carry):
        pos, t = lax.div(s, 8), lax.rem(s, 8)
        local = jnp.maximum(enc[s], 0) & 3
        for k in range(NB):
            want[t, pl.ds(pos * NB + k, 1), :] = jnp.full((1, EXC), jnp.where(local == k, 1.0, 0.0), jnp.float32)
        return carry

    lax.fori_loop(0, 64, ask, 0)
    for load in loads[:3]:
        load.wait()
    pl.semaphore_wait(barrier, len(peers))

    def remote(src, dst, ssem, rsem, where):
        return pltpu.make_async_remote_copy(
            src_ref=src, dst_ref=dst, send_sem=ssem, recv_sem=rsem,
            device_id=where, device_id_type=MESH)

    def arrives(ref, rsem):
        return remote(ref, ref, sh_s, rsem, mate).wait_recv

    def asks():
        out = [remote(want.at[partner], wanted.at[c], q_s.at[0], q_r.at[c], mate)]
        for dx in (1, 2, 3):
            out.append(remote(want.at[dx * 2 + partner], wanted2.at[dx - 1], q_s.at[6 + dx], q_r.at[7 + dx], mate))
            for k in (0, 1):
                t, back = dx * 2 + k, (NX - dx) * 2
                out.append(remote(want.at[t], wanted.at[back + c], q_s.at[t - 1], q_r.at[back + c],
                                  dev(at(dx=dx, core=k))))
        return out

    for copy in asks():
        copy.start()

    def step(n, carry):
        def mine(row):
            return pl.ds(pl.multiple_of(row * B, B), B)

        def bcast(i, lag, sem):
            piece = items.at[n, 0, i // 2, pl.ds((i % 2) * (B // 2), B // 2)]
            return remote(piece, piece, bc_s.at[sem, i], bc_r.at[n, i], dev(p, lag))

        def ring(d_from, d_to, k, dz):
            return remote(items.at[n, d_from, k], items.at[n, d_to, k], z_s.at[d_to, k],
                          z_r.at[n, d_to, k], dev(at(dz=dz)))

        def slab_start():
            return [remote(items.at[n, 0, :, pl.ds(MAIN, SLAB)], slabs.at[n, 0, NX - dx - 1], s_s.at[0, dx - 1],
                           s_r.at[n, 0, NX - dx - 1], dev(at(dx=dx))) for dx in (2, 1, 3)]

        def slab_ring(d_from, d_to, k, dz):
            half = pl.ds(2 * k, 2)
            return remote(slabs.at[n, d_from, :, half], slabs.at[n, d_to, :, half], s_s.at[d_to, k],
                          s_r.at[n, d_to, k], dev(at(dz=dz)))

        def span_of(g):
            p0, p1 = GROUPS[g]
            return pl.ds(p0, p1 - p0)

        def sends(g):
            span = span_of(g)
            out = []
            for k, dx in ((0, 1), (1, 3)):
                out.append(remote(sbuf.at[2 + k, span], rbuf.at[n, k, span], x_s.at[g, 3 + k],
                                  r_r.at[n, g, k], dev(at(dx=dx))))
            for dx in (1, 3):
                for k in (0, 1):
                    t, back = dx * 2 + k, (NX - dx) * 2 + c
                    out.append(remote(
                        sbuf.at[t - 2, span], pick.at[n, span, pl.ds(pl.multiple_of(back * B, B), MAIN)],
                        x_s.at[g, t - 1], x_r.at[n, g, back], dev(at(dx=dx, core=k))))
            out.append(remote(pbuf.at[span], pick.at[n, span, mine(c)], x_s.at[g, 0], x_r.at[n, g, c], mate))
            return out

        def slab_sends(g):
            span = span_of(g)
            return [remote(qbuf.at[dx - 1, span],
                           pick.at[n, span, pl.ds(pl.multiple_of((dx * 2 + c) * B + MAIN, SLAB), SLAB)],
                           p_s.at[g, dx - 1], p_r.at[n, g, dx - 1], mate) for dx in (1, 2, 3)]

        def relays(g):
            span = span_of(g)
            rows = pl.ds(pl.multiple_of((4 + c) * B, B), MAIN)
            return [remote(rbuf.at[n, k, span], pick.at[n, span, rows], r_s.at[g, k],
                           x_r.at[n, g, 4 + c], dev(at(dx=dx, core=k))) for k, dx in ((0, 1), (1, 3))]

        def choose(blocks, table, pos, rows):
            total = None
            for k in range(NB):
                term = blocks[k].reshape(rows // 16, 16, EXC) * onehot[table, pos * NB + k][None]
                total = term if total is None else total + term
            return total.reshape(rows, EXC)

        def pass_on(g):
            for pos in range(*GROUPS[g]):
                whole = [items[n, ORDER[pos], k] for k in range(NB)]
                head = [block[:MAIN] for block in whole]
                for t in (4, 5, 2, 3, 6, 7):
                    sbuf[t - 2, pos] = choose(head, t, pos, MAIN)
                pbuf[pos] = choose(whole, partner, pos, B)
                pick[n, pos, mine(c), :] = choose(whole, c, pos, B)
            for copy in sends(g):
                copy.start()

        def slab_pass(g):
            for pos in range(*GROUPS[g]):
                for dx in (1, 2, 3):
                    blocks = [slabs[n, ORDER[pos], dx - 1, k] for k in range(NB)]
                    qbuf[dx - 1, pos] = choose(blocks, 11 + dx - 1, pos, SLAB)
                    rows = pl.ds(pl.multiple_of((dx * 2 + c) * B + MAIN, SLAB), SLAB)
                    pick[n, pos, rows, :] = choose(blocks, 8 + dx - 1, pos, SLAB)
            for copy in slab_sends(g):
                copy.start()

        def relay(g):
            for k, copy in enumerate(relays(g)):
                arrives(rbuf.at[n, k, span_of(g)], r_r.at[n, g, k])()
                copy.start()

        def apply(g):
            span = span_of(g)
            for s in range(8):
                if s < 2:
                    pl.when(c != s)(arrives(pick.at[n, span, pl.ds(s * B, B)], x_r.at[n, g, s]))
                else:
                    arrives(pick.at[n, span, pl.ds(s * B, MAIN)], x_r.at[n, g, s])()
            for dx in (1, 2, 3):
                rows = pl.ds(pl.multiple_of((dx * 2 + partner) * B + MAIN, SLAB), SLAB)
                arrives(pick.at[n, span, rows], p_r.at[n, g, dx - 1])()
            for pos in range(*GROUPS[g]):
                term = jnp.dot(w[pos], pick[n, pos], preferred_element_type=jnp.float32)
                if pos == 0:
                    acc[...] = term
                else:
                    acc[...] += term

        first = n == 0

        @pl.when(y == 0)
        def _():
            for k in range(NB):
                rows = slice(k * B, (k + 1) * B)
                excess = inc[n, rows].astype(jnp.float32) - part[n, rows]
                solved = jnp.dot(sinv[k], excess, precision=lax.Precision.HIGHEST,
                                 preferred_element_type=jnp.float32)
                items[n, 0, k] = solved.astype(jnp.bfloat16)

        goes_up = [y <= 3, y <= 2]
        goes_down = [(y == 0) | (y >= 6), (y == 0) | (y >= 5)]
        for i in range(8):
            piece = items.at[n, 0, i // 2, pl.ds((i % 2) * (B // 2), B // 2)]
            pl.when(y != 0)(arrives(piece, bc_r.at[n, i]))
            pl.when(goes_up[i // 4])(bcast(i, up, 0).start)
            pl.when(goes_down[i // 4])(bcast(i, down, 1).start)
            if i % 2 == 1:
                ring(0, 1, i // 2, 1).start()
                ring(0, 7, i // 2, -1).start()
        for copy in slab_start():
            copy.start()

        @pl.when(first)
        def _():
            for t in range(8):
                if t < 2:
                    pl.when(c != t)(arrives(wanted.at[t], q_r.at[t]))
                else:
                    arrives(wanted.at[t], q_r.at[t])()
            wanted[c] = want[c]
            for dx in (1, 2, 3):
                arrives(wanted2.at[dx - 1], q_r.at[7 + dx])()

            def line(rows):
                return jnp.broadcast_to(rows, (16, EXC)).astype(jnp.bfloat16)

            def spread(t, carry):
                for r in range(NB * NZ):
                    onehot[t, r] = line(wanted[t, pl.ds(r, 1), :])
                return carry

            def spread_slabs(i, carry):
                for r in range(NB * NZ):
                    onehot[8 + i, r] = line(want[i * 2 + 2 + c, pl.ds(r, 1), :])
                    onehot[11 + i, r] = line(wanted2[i, pl.ds(r, 1), :])
                return carry

            lax.fori_loop(0, 8, spread, 0)
            lax.fori_loop(0, 3, spread_slabs, 0)

        pass_on(0)
        cur_out[n] = items[n, 0].reshape(OWN, EXC)
        move = remote(part.at[n], shift.at[n], sh_s, sh_r.at[n], dev(p, down))
        pl.when(y != 0)(move.start)

        def hop(make, pieces, h):
            for k in range(pieces):
                below = 2 * k < pieces
                make(h - 1, h, k, 1).wait_recv()
                if h < 3 or below:
                    make(h, h + 1, k, 1).start()
                make((9 - h) % 8, 8 - h, k, -1).wait_recv()
                if h < 3 or not below:
                    make(8 - h, 7 - h, k, -1).start()

        def last(make, pieces):
            for k in range(pieces):
                (make(3, 4, k, 1) if 2 * k < pieces else make(5, 4, k, -1)).wait_recv()

        hop(ring, 4, 1)
        pass_on(1)
        for i in range(3):
            arrives(slabs.at[n, 0, i], s_r.at[n, 0, i])()
        for k in range(2):
            slab_ring(0, 1, k, 1).start()
            slab_ring(0, 7, k, -1).start()
        hop(ring, 4, 2)
        pass_on(2)
        relay(0)
        hop(slab_ring, 2, 1)
        slab_pass(0)
        hop(ring, 4, 3)
        pass_on(3)
        relay(1)
        hop(slab_ring, 2, 2)
        slab_pass(1)

        @pl.when(first)
        def _():
            loads[3].wait()

            def place(s, carry):
                code = enc[s]
                row = jnp.where(code < 0, -1, (code >> 2) & 3)
                block = zf[jnp.maximum(code, 0) >> 4].astype(jnp.bfloat16)
                pos, col = lax.div(s, 8), lax.rem(s, 8)
                for r in range(NB):
                    keep = jnp.where(row == r, 1.0, 0.0).astype(jnp.bfloat16)
                    w[pos, pl.ds(r * B, B), pl.ds(pl.multiple_of(col * B, B), B)] = block * keep
                return carry

            lax.fori_loop(0, 64, place, 0)

        last(ring, 4)
        pass_on(4)
        relay(2)
        apply(0)
        hop(slab_ring, 2, 3)
        slab_pass(2)
        relay(3)
        apply(1)
        last(slab_ring, 2)
        slab_pass(3)
        slab_pass(4)
        relay(4)
        for g in range(2, 5):
            apply(g)

        pl.when(y != NY - 1)(move.wait_recv)

        @pl.when(y != NY - 1)
        def _():
            part[n + 1] = acc[...] + shift[n]

        @pl.when(y == NY - 1)
        def _():
            part[n + 1] = acc[...]

        for i in range(8):
            pl.when(goes_up[i // 4])(bcast(i, up, 0).wait_send)
            pl.when(goes_down[i // 4])(bcast(i, down, 1).wait_send)
        for make, pieces in ((ring, 4), (slab_ring, 2)):
            for k in range(pieces):
                for h in range(3):
                    make(h, h + 1, k, 1).wait_send()
                    make((8 - h) % 8, 7 - h, k, -1).wait_send()
                (make(3, 4, k, 1) if 2 * k < pieces else make(5, 4, k, -1)).wait_send()
        for copy in slab_start():
            copy.wait_send()
        for g in range(5):
            for copy in sends(g) + relays(g) + slab_sends(g):
                copy.wait_send()
        pl.when(y != 0)(move.wait_send)
        return carry

    lax.fori_loop(0, STEPS, step, 0)
    for copy in asks():
        copy.wait_send()
    ahead_out[0] = part[STEPS]


def body(incident, pending, self_inverse, retarded, block_rows, block_sources, owner_map):
    p = lax.axis_index("patch")
    x, z = (p // 2) % NX, p // (2 * NX)
    row = block_rows[0, 0]
    source = block_sources[0, 0]
    live = source >= 0
    storage = jnp.sum(jnp.where(source[:, None] == jnp.arange(SRC)[None, :], owner_map[None, :], 0), axis=1)
    owner, local = storage // NB, storage % NB
    d = (z - owner // (2 * NX)) % NZ
    pos = jnp.where(d == 0, 0, jnp.where(d <= 3, 2 * d - 1, jnp.where(d == 4, 7, 2 * (NZ - d))))
    column = ((owner // 2) % NX - x) % NX * 2 + owner % 2
    slot = pos * 8 + column
    code = jnp.arange(LIST, dtype=jnp.int32) * 16 + row * 4 + local
    hit = (slot[None, :] == jnp.arange(64)[:, None]) & live[None, :]
    enc = jnp.max(jnp.where(hit, code[None, :], -1), axis=1).astype(jnp.int32)
    vmem = pl.BlockSpec(memory_space=pltpu.VMEM)
    hbm = pl.BlockSpec(memory_space=pltpu.HBM)
    dma = pltpu.SemaphoreType.DMA
    return pl.pallas_call(
        kernel,
        out_shape=(jax.ShapeDtypeStruct((STEPS, OWN, EXC), jnp.bfloat16),
                   jax.ShapeDtypeStruct((1, OWN, EXC), jnp.float32)),
        in_specs=[pl.BlockSpec(memory_space=pltpu.SMEM), hbm, hbm, hbm, hbm],
        out_specs=(vmem, vmem),
        scratch_shapes=[
            pltpu.VMEM((STEPS, OWN, EXC), jnp.bfloat16),
            pltpu.VMEM((NB, B, B), jnp.float32),
            pltpu.VMEM((LIST, B, B), jnp.float32),
            pltpu.VMEM((NZ, OWN, 8 * B), jnp.bfloat16),
            pltpu.VMEM((STEPS, NZ, NB, B, EXC), jnp.bfloat16),
            pltpu.VMEM((STEPS, NZ, NX - 1, NB, SLAB, EXC), jnp.bfloat16),
            pltpu.VMEM((STEPS, NZ, 8 * B, EXC), jnp.bfloat16),
            pltpu.VMEM((6, NZ, MAIN, EXC), jnp.bfloat16),
            pltpu.VMEM((NZ, B, EXC), jnp.bfloat16),
            pltpu.VMEM((NX - 1, NZ, SLAB, EXC), jnp.bfloat16),
            pltpu.VMEM((STEPS, 2, NZ, MAIN, EXC), jnp.bfloat16),
            pltpu.VMEM((STEPS + 1, OWN, EXC), jnp.float32),
            pltpu.VMEM((STEPS, OWN, EXC), jnp.float32),
            pltpu.VMEM((OWN, EXC), jnp.float32),
            pltpu.VMEM((8, NZ * NB, EXC), jnp.float32),
            pltpu.VMEM((8, NZ * NB, EXC), jnp.float32),
            pltpu.VMEM((NX - 1, NZ * NB, EXC), jnp.float32),
            pltpu.VMEM((14, NZ * NB, 16, EXC), jnp.bfloat16),
            dma((4,)), dma((STEPS, 8)), dma((STEPS, NZ, 4)), dma((STEPS, NZ, 3)), dma((STEPS, 5, 8)), dma((STEPS, 5, 2)),
            dma((STEPS, 5, 3)), dma((STEPS,)), dma((11,)),
            dma((2, 8)), dma((NZ, 4)), dma((NZ, 3)), dma((5, 7)), dma((5, 2)), dma((5, 3)), dma, dma((10,)),
        ],
        compiler_params=pltpu.CompilerParams(collective_id=0, has_side_effects=True,
                                             vmem_limit_bytes=48 * 1024 * 1024),
    )(enc, *(pltpu.with_memory_space_constraint(a, pltpu.HBM) for a in (incident, pending, self_inverse, retarded)))


def solution(mesh):
    in_specs = (
        P(None, "patch", None),
        P("lag", "patch", None),
        P("patch", None, None),
        P("lag", "patch", None, None, None),
        P("lag", "patch", None),
        P("lag", "patch", None),
        P(),
    )
    out_specs = (P(None, "patch", None), P("lag", "patch", None))
    return jax.shard_map(body, mesh=mesh, in_specs=in_specs, out_specs=out_specs, check_vma=False)
```

```python
import jax
import jax.numpy as jnp
from jax import lax
from jax.experimental import pallas as pl
from jax.experimental.pallas import tpu as pltpu
from jax.sharding import PartitionSpec as P

EXC = 128
B = 128
NB = 4
OWN = NB * B
STEPS = 4
LIST = 56
SRC = 256
NX, NZ, NY = 4, 8, 8
MESH = pl.DeviceIdType.MESH

ORDER = (0, 1, 7, 2, 6, 3, 5, 4)
GROUPS = ((0, 1), (1, 3), (3, 5), (5, 7), (7, 8))
HALF = B // 2
MAIN, SLAB = 48, 16


def kernel(enc, inc_hbm, pend_hbm, sinv_hbm, zmat, cur_out, ahead_out,
           inc, pend, sinv, zf, w, items, slabs, pick, sbuf, pbuf, qbuf, rbuf, part, shift, acc, want, wanted, wanted2, onehot,
           load_sem, bc_r, z_r, s_r, x_r, r_r, p_r, sh_r, q_r,
           bc_s, z_s, s_s, x_s, r_s, p_s, sh_s, q_s):
    y = lax.axis_index("lag")
    p = lax.axis_index("patch")
    c = lax.rem(p, 2)
    x = lax.rem(lax.div(p, 2), NX)
    z = lax.div(p, 2 * NX)

    def at(dx=0, dz=0, core=None):
        core = c if core is None else core
        return lax.rem(z + dz + NZ, NZ) * (2 * NX) + lax.rem(x + dx, NX) * 2 + core

    def dev(patch, lag=None):
        return {"lag": y if lag is None else lag, "patch": patch}

    up, down = lax.rem(y + 1, NY), lax.rem(y + NY - 1, NY)
    partner = 1 - c
    mate = dev(at(core=partner))
    peers = [dev(at(dz=1)), dev(at(dz=-1)), mate, dev(p, up), dev(p, down)]
    peers += [dev(at(dx=dx, core=k)) for dx in (1, 2, 3) for k in (0, 1)]

    loads = [pltpu.make_async_copy(pend_hbm.at[0], pend, load_sem.at[0]),
             pltpu.make_async_copy(inc_hbm, inc, load_sem.at[1]),
             pltpu.make_async_copy(sinv_hbm, sinv, load_sem.at[2]),
             pltpu.make_async_copy(zmat.at[0, 0], zf, load_sem.at[3])]

    barrier = pltpu.get_barrier_semaphore()
    for peer in peers:
        pl.semaphore_signal(barrier, inc=1, device_id=peer, device_id_type=MESH)
    for load in loads:
        load.start()

    def ask(s, carry):
        pos, t = lax.div(s, 8), lax.rem(s, 8)
        local = jnp.maximum(enc[s], 0) & 3
        for k in range(NB):
            want[t, pl.ds(pos * NB + k, 1), :] = jnp.full((1, EXC), jnp.where(local == k, 1.0, 0.0), jnp.float32)
        return carry

    lax.fori_loop(0, 64, ask, 0)
    for load in loads[:3]:
        load.wait()
    low = lax.broadcasted_iota(jnp.int32, (OWN // 2, EXC), 1) < HALF
    low_b = low[:B]
    low_h = low[:HALF]

    def roll(v):
        return pltpu.roll(v, HALF, 1)

    top, bottom = pend[: OWN // 2], pend[OWN // 2 :]
    part[0, 0] = jnp.where(low, top, roll(bottom))
    part[1, 0] = jnp.where(low, roll(top), bottom)
    pl.semaphore_wait(barrier, len(peers))

    def remote(src, dst, ssem, rsem, where):
        return pltpu.make_async_remote_copy(
            src_ref=src, dst_ref=dst, send_sem=ssem, recv_sem=rsem,
            device_id=where, device_id_type=MESH)

    def arrives(ref, rsem):
        return remote(ref, ref, sh_s.at[0], rsem, mate).wait_recv

    def asks():
        out = [remote(want.at[partner], wanted.at[c], q_s.at[0], q_r.at[c], mate)]
        for dx in (1, 2, 3):
            out.append(remote(want.at[dx * 2 + partner], wanted2.at[dx - 1], q_s.at[6 + dx], q_r.at[7 + dx], mate))
            for k in (0, 1):
                t, back = dx * 2 + k, (NX - dx) * 2
                out.append(remote(want.at[t], wanted.at[back + c], q_s.at[t - 1], q_r.at[back + c],
                                  dev(at(dx=dx, core=k))))
        return out

    for copy in asks():
        copy.start()

    def chain(n, h):
        def bcast(i, lag, sem):
            piece = items.at[n, h, 0, i]
            return remote(piece, piece, bc_s.at[h, sem, i], bc_r.at[n, h, i], dev(p, lag))

        def ring(d_from, d_to, k, dz):
            half = pl.ds(2 * k, 2)
            return remote(items.at[n, h, d_from, half], items.at[n, h, d_to, half], z_s.at[h, d_to, k],
                          z_r.at[n, h, d_to, k], dev(at(dz=dz)))

        def slab_start():
            return [remote(items.at[n, h, 0, :, pl.ds(MAIN, SLAB)], slabs.at[n, h, 0, NX - dx - 1],
                           s_s.at[h, 0, dx - 1], s_r.at[n, h, 0, NX - dx - 1], dev(at(dx=dx))) for dx in (2, 1, 3)]

        def slab_ring(d_from, d_to, k, dz):
            half = pl.ds(2 * k, 2)
            return remote(slabs.at[n, h, d_from, :, half], slabs.at[n, h, d_to, :, half], s_s.at[h, d_to, k],
                          s_r.at[n, h, d_to, k], dev(at(dz=dz)))

        def span_of(g):
            p0, p1 = GROUPS[g]
            return pl.ds(p0, p1 - p0)

        def rows_of(slot, offset, size):
            return pl.ds(pl.multiple_of(slot * HALF + offset, 16), size)

        def sends(g):
            span = span_of(g)
            out = []
            for k, dx in ((0, 1), (1, 3)):
                out.append(remote(sbuf.at[h, 2 + k, span], rbuf.at[n, h, k, span], x_s.at[h, g, 3 + k],
                                  r_r.at[n, h, g, k], dev(at(dx=dx))))
            for dx in (1, 3):
                for k in (0, 1):
                    t, back = dx * 2 + k, (NX - dx) * 2 + c
                    out.append(remote(
                        sbuf.at[h, t - 2, span], pick.at[n, h, span, rows_of(back, 0, MAIN)],
                        x_s.at[h, g, t - 1], x_r.at[n, h, g, back], dev(at(dx=dx, core=k))))
            out.append(remote(pbuf.at[h, span], pick.at[n, h, span, rows_of(c, 0, HALF)], x_s.at[h, g, 0],
                              x_r.at[n, h, g, c], mate))
            return out

        def slab_sends(g):
            span = span_of(g)
            return [remote(qbuf.at[h, dx - 1, span], pick.at[n, h, span, rows_of(dx * 2 + c, MAIN, SLAB)],
                           p_s.at[h, g, dx - 1], p_r.at[n, h, g, dx - 1], mate) for dx in (1, 2, 3)]

        def relays(g):
            span = span_of(g)
            return [remote(rbuf.at[n, h, k, span], pick.at[n, h, span, rows_of(4 + c, 0, MAIN)], r_s.at[h, g, k],
                           x_r.at[n, h, g, 4 + c], dev(at(dx=dx, core=k))) for k, dx in ((0, 1), (1, 3))]

        def choose(blocks, table, pos, rows):
            total = None
            for k in range(NB):
                term = blocks[k].reshape(rows // 16, 16, EXC) * onehot[table, pos * NB + k][None]
                total = term if total is None else total + term
            return total.reshape(rows, EXC)

        def pass_on(g):
            for pos in range(*GROUPS[g]):
                whole = [items[n, h, ORDER[pos], k] for k in range(NB)]
                head = [block[:MAIN] for block in whole]
                for t in (4, 5, 2, 3, 6, 7):
                    sbuf[h, t - 2, pos] = choose(head, t, pos, MAIN)
                pbuf[h, pos] = choose(whole, partner, pos, HALF)
                pick[n, h, pos, rows_of(c, 0, HALF), :] = choose(whole, c, pos, HALF)
            for copy in sends(g):
                copy.start()

        def slab_pass(g):
            for pos in range(*GROUPS[g]):
                for dx in (1, 2, 3):
                    blocks = [slabs[n, h, ORDER[pos], dx - 1, k] for k in range(NB)]
                    qbuf[h, dx - 1, pos] = choose(blocks, 11 + dx - 1, pos, SLAB)
                    pick[n, h, pos, rows_of(dx * 2 + c, MAIN, SLAB), :] = choose(blocks, 8 + dx - 1, pos, SLAB)
            for copy in slab_sends(g):
                copy.start()

        def relay(g):
            for k, copy in enumerate(relays(g)):
                arrives(rbuf.at[n, h, k, span_of(g)], r_r.at[n, h, g, k])()
                copy.start()

        def apply(g):
            span = span_of(g)
            for s in range(8):
                if s < 2:
                    pl.when(c != s)(arrives(pick.at[n, h, span, pl.ds(s * HALF, HALF)], x_r.at[n, h, g, s]))
                else:
                    arrives(pick.at[n, h, span, pl.ds(s * HALF, MAIN)], x_r.at[n, h, g, s])()
            for dx in (1, 2, 3):
                arrives(pick.at[n, h, span, rows_of(dx * 2 + partner, MAIN, SLAB)], p_r.at[n, h, g, dx - 1])()
            for pos in range(*GROUPS[g]):
                term = jnp.dot(w[pos], pick[n, h, pos], preferred_element_type=jnp.float32)
                if pos == 0:
                    acc[h] = term
                else:
                    acc[h] += term

        def hop(make, i):
            for k in range(2):
                make(i - 1, i, k, 1).wait_recv()
                if i < 3 or k == 0:
                    make(i, i + 1, k, 1).start()
                make((9 - i) % 8, 8 - i, k, -1).wait_recv()
                if i < 3 or k == 1:
                    make(8 - i, 7 - i, k, -1).start()

        def last(make):
            make(3, 4, 0, 1).wait_recv()
            make(5, 4, 1, -1).wait_recv()

        move = remote(part.at[h, n], shift.at[h, n], sh_s.at[h], sh_r.at[n, h], dev(p, down))
        goes_up = [y <= 3, y <= 2]
        goes_down = [(y == 0) | (y >= 6), (y == 0) | (y >= 5)]

        def begin():
            @pl.when(y == 0)
            def _():
                for j in range(2):
                    rows = pl.ds(j * B, B)
                    left, right = inc[n, rows].astype(jnp.float32), inc[n, pl.ds(2 * B + j * B, B)].astype(jnp.float32)
                    if h == 0:
                        due = jnp.where(low_b, left, roll(right))
                    else:
                        due = jnp.where(low_b, roll(left), right)
                    excess = due - part[h, n, rows]
                    for k in (j, j + 2):
                        solved = jnp.dot(sinv[k], excess, precision=lax.Precision.HIGHEST,
                                         preferred_element_type=jnp.float32)
                        first_rows, last_rows = solved[:HALF], solved[HALF:]
                        if k == j:
                            packed = jnp.where(low_h, first_rows, roll(last_rows))
                        else:
                            packed = jnp.where(low_h, roll(first_rows), last_rows)
                        items[n, h, 0, k] = packed.astype(jnp.bfloat16)

            for i in range(NB):
                pl.when(y != 0)(arrives(items.at[n, h, 0, i], bc_r.at[n, h, i]))
                pl.when(goes_up[i // 2])(bcast(i, up, 0).start)
                pl.when(goes_down[i // 2])(bcast(i, down, 1).start)
                if i % 2 == 1:
                    ring(0, 1, i // 2, 1).start()
                    ring(0, 7, i // 2, -1).start()
            for copy in slab_start():
                copy.start()
            if h == 0:
                pl.when(n == 0)(tables)
            pass_on(0)
            pl.when(y != 0)(move.start)
            if h == 1:
                for k in range(NB):
                    a, b = items[n, 0, 0, k].astype(jnp.float32), items[n, 1, 0, k].astype(jnp.float32)
                    cur_out[n, pl.ds(k * B, HALF)] = jnp.where(low_h, a, roll(b)).astype(jnp.bfloat16)
                    cur_out[n, pl.ds(k * B + HALF, HALF)] = jnp.where(low_h, roll(a), b).astype(jnp.bfloat16)

        def stage1():
            hop(ring, 1)
            pass_on(1)
            for i in range(3):
                arrives(slabs.at[n, h, 0, i], s_r.at[n, h, 0, i])()
            for k in range(2):
                slab_ring(0, 1, k, 1).start()
                slab_ring(0, 7, k, -1).start()

        def stage2():
            hop(ring, 2)
            pass_on(2)
            relay(0)

        def stage3():
            hop(slab_ring, 1)
            slab_pass(0)
            hop(ring, 3)
            pass_on(3)
            relay(1)

        def stage4():
            hop(slab_ring, 2)
            slab_pass(1)
            last(ring)
            pass_on(4)
            relay(2)
            if h == 0:
                pl.when(n == 0)(operator)

        def stage5():
            apply(0)
            hop(slab_ring, 3)
            slab_pass(2)
            relay(3)

        def stage6():
            apply(1)
            apply(2)
            last(slab_ring)
            slab_pass(3)
            slab_pass(4)
            relay(4)

        def finish():
            apply(3)
            apply(4)
            fresh = acc[h, pl.ds(0, OWN)] + roll(acc[h, pl.ds(OWN, OWN)])
            packed = jnp.where(low, fresh[: OWN // 2], roll(fresh[OWN // 2 :]))
            pl.when(y != NY - 1)(move.wait_recv)

            @pl.when(y != NY - 1)
            def _():
                part[h, n + 1] = packed + shift[h, n]

            @pl.when(y == NY - 1)
            def _():
                part[h, n + 1] = packed

            for i in range(NB):
                pl.when(goes_up[i // 2])(bcast(i, up, 0).wait_send)
                pl.when(goes_down[i // 2])(bcast(i, down, 1).wait_send)
            for make in (ring, slab_ring):
                for k in range(2):
                    for i in range(3):
                        make(i, i + 1, k, 1).wait_send()
                        make((8 - i) % 8, 7 - i, k, -1).wait_send()
                make(3, 4, 0, 1).wait_send()
                make(5, 4, 1, -1).wait_send()
            for copy in slab_start():
                copy.wait_send()
            for g in range(5):
                for copy in sends(g) + relays(g) + slab_sends(g):
                    copy.wait_send()
            pl.when(y != 0)(move.wait_send)

        return [begin, stage1, stage2, stage3, stage4, stage5, stage6, finish]

    def tables():
        for t in range(8):
            if t < 2:
                pl.when(c != t)(arrives(wanted.at[t], q_r.at[t]))
            else:
                arrives(wanted.at[t], q_r.at[t])()
        wanted[c] = want[c]
        for dx in (1, 2, 3):
            arrives(wanted2.at[dx - 1], q_r.at[7 + dx])()

        def line(rows):
            return jnp.broadcast_to(rows, (16, EXC)).astype(jnp.bfloat16)

        def spread(t, carry):
            for r in range(NB * NZ):
                onehot[t, r] = line(wanted[t, pl.ds(r, 1), :])
            return carry

        def spread_slabs(i, carry):
            for r in range(NB * NZ):
                onehot[8 + i, r] = line(want[i * 2 + 2 + c, pl.ds(r, 1), :])
                onehot[11 + i, r] = line(wanted2[i, pl.ds(r, 1), :])
            return carry

        lax.fori_loop(0, 8, spread, 0)
        lax.fori_loop(0, 3, spread_slabs, 0)

    def operator():
        loads[3].wait()

        def place(pair, carry):
            pos, col = lax.div(pair, 4), lax.rem(pair, 4)
            codes = [enc[2 * pair], enc[2 * pair + 1]]
            rows = [jnp.where(code < 0, -1, (code >> 2) & 3) for code in codes]
            even, odd = [zf[jnp.maximum(code, 0) >> 4] for code in codes]
            even_turned, odd_turned = roll(even), roll(odd)
            lanes = pl.ds(pl.multiple_of(col * B, B), B)
            for r in range(NB):
                keep = [jnp.where(row == r, 1.0, 0.0) for row in rows]
                w[pos, pl.ds(r * B, B), lanes] = jnp.where(
                    low_b, even * keep[0], odd_turned * keep[1]).astype(jnp.bfloat16)
                w[pos, pl.ds(OWN + r * B, B), lanes] = jnp.where(
                    low_b, even_turned * keep[0], odd * keep[1]).astype(jnp.bfloat16)
            return carry

        lax.fori_loop(0, 32, place, 0)

    def step(n, carry):
        ahead, behind, late = chain(n, 0), chain(n, 1), chain(n - 1, 1)
        for i in range(4):
            pl.when(n < STEPS)(ahead[i])
            pl.when(n > 0)(late[i + 4])
        for i in range(4):
            pl.when(n < STEPS)(ahead[i + 4])
            pl.when(n < STEPS)(behind[i])
        return carry

    lax.fori_loop(0, STEPS + 1, step, 0)
    for copy in asks():
        copy.wait_send()
    a, b = part[0, STEPS], part[1, STEPS]
    ahead_out[0, pl.ds(0, OWN // 2)] = jnp.where(low, a, roll(b))
    ahead_out[0, pl.ds(OWN // 2, OWN // 2)] = jnp.where(low, roll(a), b)


def body(incident, pending, self_inverse, retarded, block_rows, block_sources, owner_map):
    p = lax.axis_index("patch")
    x, z = (p // 2) % NX, p // (2 * NX)
    row = block_rows[0, 0]
    source = block_sources[0, 0]
    live = source >= 0
    storage = jnp.sum(jnp.where(source[:, None] == jnp.arange(SRC)[None, :], owner_map[None, :], 0), axis=1)
    owner, local = storage // NB, storage % NB
    d = (z - owner // (2 * NX)) % NZ
    pos = jnp.where(d == 0, 0, jnp.where(d <= 3, 2 * d - 1, jnp.where(d == 4, 7, 2 * (NZ - d))))
    column = ((owner // 2) % NX - x) % NX * 2 + owner % 2
    slot = pos * 8 + column
    code = jnp.arange(LIST, dtype=jnp.int32) * 16 + row * 4 + local
    hit = (slot[None, :] == jnp.arange(64)[:, None]) & live[None, :]
    enc = jnp.max(jnp.where(hit, code[None, :], -1), axis=1).astype(jnp.int32)
    vmem = pl.BlockSpec(memory_space=pltpu.VMEM)
    hbm = pl.BlockSpec(memory_space=pltpu.HBM)
    dma = pltpu.SemaphoreType.DMA
    return pl.pallas_call(
        kernel,
        out_shape=(jax.ShapeDtypeStruct((STEPS, OWN, EXC), jnp.bfloat16),
                   jax.ShapeDtypeStruct((1, OWN, EXC), jnp.float32)),
        in_specs=[pl.BlockSpec(memory_space=pltpu.SMEM), hbm, hbm, hbm, hbm],
        out_specs=(vmem, vmem),
        scratch_shapes=[
            pltpu.VMEM((STEPS, OWN, EXC), jnp.bfloat16),
            pltpu.VMEM((OWN, EXC), jnp.float32),
            pltpu.VMEM((NB, B, B), jnp.float32),
            pltpu.VMEM((LIST, B, B), jnp.float32),
            pltpu.VMEM((NZ, 2 * OWN, 8 * HALF), jnp.bfloat16),
            pltpu.VMEM((STEPS, 2, NZ, NB, HALF, EXC), jnp.bfloat16),
            pltpu.VMEM((STEPS, 2, NZ, NX - 1, NB, SLAB, EXC), jnp.bfloat16),
            pltpu.VMEM((STEPS, 2, NZ, 8 * HALF, EXC), jnp.bfloat16),
            pltpu.VMEM((2, 6, NZ, MAIN, EXC), jnp.bfloat16),
            pltpu.VMEM((2, NZ, HALF, EXC), jnp.bfloat16),
            pltpu.VMEM((2, NX - 1, NZ, SLAB, EXC), jnp.bfloat16),
            pltpu.VMEM((STEPS, 2, 2, NZ, MAIN, EXC), jnp.bfloat16),
            pltpu.VMEM((2, STEPS + 1, OWN // 2, EXC), jnp.float32),
            pltpu.VMEM((2, STEPS, OWN // 2, EXC), jnp.float32),
            pltpu.VMEM((2, 2 * OWN, EXC), jnp.float32),
            pltpu.VMEM((8, NZ * NB, EXC), jnp.float32),
            pltpu.VMEM((8, NZ * NB, EXC), jnp.float32),
            pltpu.VMEM((NX - 1, NZ * NB, EXC), jnp.float32),
            pltpu.VMEM((14, NZ * NB, 16, EXC), jnp.bfloat16),
            dma((4,)), dma((STEPS, 2, NB)), dma((STEPS, 2, NZ, 2)), dma((STEPS, 2, NZ, 3)), dma((STEPS, 2, 5, 8)),
            dma((STEPS, 2, 5, 2)), dma((STEPS, 2, 5, 3)), dma((STEPS, 2)), dma((11,)),
            dma((2, 2, NB)), dma((2, NZ, 2)), dma((2, NZ, 3)), dma((2, 5, 7)), dma((2, 5, 2)), dma((2, 5, 3)),
            dma((2,)), dma((10,)),
        ],
        compiler_params=pltpu.CompilerParams(collective_id=0, has_side_effects=True,
                                             vmem_limit_bytes=48 * 1024 * 1024),
    )(enc, *(pltpu.with_memory_space_constraint(a, pltpu.HBM) for a in (incident, pending, self_inverse, retarded)))


def solution(mesh):
    in_specs = (
        P(None, "patch", None),
        P("lag", "patch", None),
        P("patch", None, None),
        P("lag", "patch", None, None, None),
        P("lag", "patch", None),
        P("lag", "patch", None),
        P(),
    )
    out_specs = (P(None, "patch", None), P("lag", "patch", None))
    return jax.shard_map(body, mesh=mesh, in_specs=in_specs, out_specs=out_specs, check_vma=False)
```

```python
import jax
import jax.numpy as jnp
from jax import lax
from jax.experimental import pallas as pl
from jax.experimental.pallas import tpu as pltpu
from jax.sharding import PartitionSpec as P

EXC = 128
B = 128
NB = 4
OWN = NB * B
STEPS = 4
LIST = 56
SRC = 256
NX, NZ, NY = 4, 8, 8
MESH = pl.DeviceIdType.MESH

ORDER = (0, 1, 7, 2, 6, 3, 5, 4)
GROUPS = ((0, 1), (1, 3), (3, 5), (5, 7), (7, 8))
MAIN, SLAB = 96, 32


def kernel(enc, inc_hbm, pend, sinv_hbm, zmat, cur_out, ahead_out,
           inc, sinv, zf, w, items, slabs, pick, sbuf, pbuf, qbuf, part, shift, acc, want, wanted, wanted2, onehot,
           load_sem, bc_r, z_r, s_r, x_r, p_r, sh_r, q_r,
           bc_s, z_s, s_s, x_s, p_s, sh_s, q_s):
    y = lax.axis_index("lag")
    p = lax.axis_index("patch")
    c = lax.rem(p, 2)
    x = lax.rem(lax.div(p, 2), NX)
    z = lax.div(p, 2 * NX)

    def at(dx=0, dz=0, core=None):
        core = c if core is None else core
        return lax.rem(z + dz + NZ, NZ) * (2 * NX) + lax.rem(x + dx, NX) * 2 + core

    def dev(patch, lag=None):
        return {"lag": y if lag is None else lag, "patch": patch}

    up, down = lax.rem(y + 1, NY), lax.rem(y + NY - 1, NY)
    up2, down2 = lax.rem(y + 2, NY), lax.rem(y + NY - 2, NY)
    partner = 1 - c
    mate = dev(at(core=partner))
    peers = [dev(at(dz=1)), dev(at(dz=-1)), mate, dev(p, up), dev(p, down), dev(p, up2), dev(p, down2)]
    peers += [dev(at(dx=dx, core=k)) for dx in (1, 2, 3) for k in (0, 1)]

    loads = [pltpu.make_async_copy(pend.at[0], part.at[0], load_sem.at[0]),
             pltpu.make_async_copy(inc_hbm, inc, load_sem.at[1]),
             pltpu.make_async_copy(sinv_hbm, sinv, load_sem.at[2]),
             pltpu.make_async_copy(zmat.at[0, 0], zf, load_sem.at[3])]

    barrier = pltpu.get_barrier_semaphore()
    for peer in peers:
        pl.semaphore_signal(barrier, inc=1, device_id=peer, device_id_type=MESH)
    for load in loads:
        load.start()

    def ask(s, carry):
        pos, t = lax.div(s, 8), lax.rem(s, 8)
        local = jnp.maximum(enc[s], 0) & 3
        for k in range(NB):
            want[t, pl.ds(pos * NB + k, 1), :] = jnp.full((1, EXC), jnp.where(local == k, 1.0, 0.0), jnp.float32)
        return carry

    lax.fori_loop(0, 64, ask, 0)
    for load in loads:
        load.wait()

    def place(s, carry):
        code = enc[s]
        row = jnp.where(code < 0, -1, (code >> 2) & 3)
        block = zf[jnp.maximum(code, 0) >> 4].astype(jnp.bfloat16)
        pos, col = lax.div(s, 8), lax.rem(s, 8)
        for r in range(NB):
            keep = jnp.where(row == r, 1.0, 0.0).astype(jnp.bfloat16)
            w[pos, pl.ds(r * B, B), pl.ds(pl.multiple_of(col * B, B), B)] = block * keep
        return carry

    lax.fori_loop(0, 64, place, 0)
    pl.semaphore_wait(barrier, len(peers))

    def remote(src, dst, ssem, rsem, where):
        return pltpu.make_async_remote_copy(
            src_ref=src, dst_ref=dst, send_sem=ssem, recv_sem=rsem,
            device_id=where, device_id_type=MESH)

    def arrives(ref, rsem):
        return remote(ref, ref, sh_s, rsem, mate).wait_recv

    def asks():
        out = [remote(want.at[partner], wanted.at[c], q_s.at[0], q_r.at[c], mate)]
        for dx in (1, 2, 3):
            out.append(remote(want.at[dx * 2 + partner], wanted2.at[dx - 1], q_s.at[6 + dx], q_r.at[7 + dx], mate))
            for k in (0, 1):
                t, back = dx * 2 + k, (NX - dx) * 2
                out.append(remote(want.at[t], wanted.at[back + c], q_s.at[t - 1], q_r.at[back + c],
                                  dev(at(dx=dx, core=k))))
        return out

    for copy in asks():
        copy.start()

    def step(n, carry):
        def mine(row):
            return pl.ds(pl.multiple_of(row * B, B), B)

        def piece(i):
            return items.at[n, 0, i // 2, pl.ds((i % 2) * (B // 2), B // 2)]

        def bcast(i, way):
            lag = (up2, down2, up, down)[way]
            goes = ((y == 0) | ((y == 2) & (i < 4)), (y == 0) | ((y == 6) & (i >= 4)),
                    (y == 0) | (y == 2), (y == 0) | (y == 6))[way]
            return goes, remote(piece(i), piece(i), bc_s.at[way, i], bc_r.at[n, i], dev(p, lag))

        def ring(d_from, d_to, k, dz):
            return remote(items.at[n, d_from, k], items.at[n, d_to, k], z_s.at[d_to, k],
                          z_r.at[n, d_to, k], dev(at(dz=dz)))

        def slab_start():
            return [remote(items.at[n, 0, :, pl.ds(MAIN, SLAB)], slabs.at[n, 0, NX - dx - 1], s_s.at[0, dx - 1],
                           s_r.at[n, 0, NX - dx - 1], dev(at(dx=dx))) for dx in (2, 1, 3)]

        def slab_ring(d_from, d_to, k, dz):
            half = pl.ds(2 * k, 2)
            return remote(slabs.at[n, d_from, :, half], slabs.at[n, d_to, :, half], s_s.at[d_to, k],
                          s_r.at[n, d_to, k], dev(at(dz=dz)))

        def span_of(g):
            p0, p1 = GROUPS[g]
            return pl.ds(p0, p1 - p0)

        def sends(g):
            span = span_of(g)
            out = []
            for k in (0, 1):
                out.append(remote(sbuf.at[2 + k, span],
                                  pick.at[n, span, pl.ds(pl.multiple_of((4 + c) * B, B), MAIN)],
                                  x_s.at[g, 3 + k], x_r.at[n, g, 4 + c], dev(at(dx=2, core=k))))
            for dx in (1, 3):
                for k in (0, 1):
                    t, back = dx * 2 + k, (NX - dx) * 2 + c
                    out.append(remote(
                        sbuf.at[t - 2, span], pick.at[n, span, pl.ds(pl.multiple_of(back * B, B), MAIN)],
                        x_s.at[g, t - 1], x_r.at[n, g, back], dev(at(dx=dx, core=k))))
            out.append(remote(pbuf.at[span], pick.at[n, span, mine(c)], x_s.at[g, 0], x_r.at[n, g, c], mate))
            return out

        def slab_sends(g):
            span = span_of(g)
            return [remote(qbuf.at[dx - 1, span],
                           pick.at[n, span, pl.ds(pl.multiple_of((dx * 2 + c) * B + MAIN, SLAB), SLAB)],
                           p_s.at[g, dx - 1], p_r.at[n, g, dx - 1], mate) for dx in (1, 2, 3)]

        def choose(blocks, table, pos, rows):
            total = None
            for k in range(NB):
                term = blocks[k].reshape(rows // 16, 16, EXC) * onehot[table, pos * NB + k][None]
                total = term if total is None else total + term
            return total.reshape(rows, EXC)

        def pass_on(g):
            for pos in range(*GROUPS[g]):
                whole = [items[n, ORDER[pos], k] for k in range(NB)]
                head = [block[:MAIN] for block in whole]
                for t in (4, 5, 2, 3, 6, 7):
                    sbuf[t - 2, pos] = choose(head, t, pos, MAIN)
                pbuf[pos] = choose(whole, partner, pos, B)
                pick[n, pos, mine(c), :] = choose(whole, c, pos, B)
            for copy in sends(g):
                copy.start()

        def slab_pass(g):
            for pos in range(*GROUPS[g]):
                for dx in (1, 2, 3):
                    blocks = [slabs[n, ORDER[pos], dx - 1, k] for k in range(NB)]
                    qbuf[dx - 1, pos] = choose(blocks, 11 + dx - 1, pos, SLAB)
                    rows = pl.ds(pl.multiple_of((dx * 2 + c) * B + MAIN, SLAB), SLAB)
                    pick[n, pos, rows, :] = choose(blocks, 8 + dx - 1, pos, SLAB)
            for copy in slab_sends(g):
                copy.start()

        def apply(g):
            span = span_of(g)
            for s in range(8):
                if s < 2:
                    pl.when(c != s)(arrives(pick.at[n, span, pl.ds(s * B, B)], x_r.at[n, g, s]))
                else:
                    arrives(pick.at[n, span, pl.ds(s * B, MAIN)], x_r.at[n, g, s])()
            for dx in (1, 2, 3):
                rows = pl.ds(pl.multiple_of((dx * 2 + partner) * B + MAIN, SLAB), SLAB)
                arrives(pick.at[n, span, rows], p_r.at[n, g, dx - 1])()
            for pos in range(*GROUPS[g]):
                term = jnp.dot(w[pos], pick[n, pos], preferred_element_type=jnp.float32)
                if pos == 0:
                    acc[...] = term
                else:
                    acc[...] += term

        first = n == 0

        @pl.when(y == 0)
        def _():
            for k in range(NB):
                rows = slice(k * B, (k + 1) * B)
                excess = inc[n, rows].astype(jnp.float32) - part[n, rows]
                solved = jnp.dot(sinv[k], excess, precision=lax.Precision.HIGHEST,
                                 preferred_element_type=jnp.float32)
                items[n, 0, k] = solved.astype(jnp.bfloat16)

        for k in range(NB):
            for i in (2 * k, 2 * k + 1):
                pl.when(y != 0)(arrives(piece(i), bc_r.at[n, i]))
                for way in (0, 1):
                    goes, copy = bcast(i, way)
                    pl.when(goes)(copy.start)
            ring(0, 1, k, 1).start()
            ring(0, 7, k, -1).start()
        for i in range(8):
            for way in (2, 3):
                goes, copy = bcast(i, way)
                pl.when(goes)(copy.start)
        for copy in slab_start():
            copy.start()

        @pl.when(first)
        def _():
            for t in range(8):
                if t < 2:
                    pl.when(c != t)(arrives(wanted.at[t], q_r.at[t]))
                else:
                    arrives(wanted.at[t], q_r.at[t])()
            wanted[c] = want[c]
            for dx in (1, 2, 3):
                arrives(wanted2.at[dx - 1], q_r.at[7 + dx])()

            def line(rows):
                return jnp.broadcast_to(rows, (16, EXC)).astype(jnp.bfloat16)

            def spread(t, carry):
                for r in range(NB * NZ):
                    onehot[t, r] = line(wanted[t, pl.ds(r, 1), :])
                return carry

            def spread_slabs(i, carry):
                for r in range(NB * NZ):
                    onehot[8 + i, r] = line(want[i * 2 + 2 + c, pl.ds(r, 1), :])
                    onehot[11 + i, r] = line(wanted2[i, pl.ds(r, 1), :])
                return carry

            lax.fori_loop(0, 8, spread, 0)
            lax.fori_loop(0, 3, spread_slabs, 0)

        pass_on(0)
        cur_out[n] = items[n, 0].reshape(OWN, EXC)
        move = remote(part.at[n], shift.at[n], sh_s, sh_r.at[n], dev(p, down))
        pl.when(y != 0)(move.start)

        def hop(make, pieces, h):
            for k in range(pieces):
                below = 2 * k < pieces
                make(h - 1, h, k, 1).wait_recv()
                if h < 3 or below:
                    make(h, h + 1, k, 1).start()
                make((9 - h) % 8, 8 - h, k, -1).wait_recv()
                if h < 3 or not below:
                    make(8 - h, 7 - h, k, -1).start()

        def last(make, pieces):
            for k in range(pieces):
                (make(3, 4, k, 1) if 2 * k < pieces else make(5, 4, k, -1)).wait_recv()

        hop(ring, 4, 1)
        pass_on(1)
        for i in range(3):
            arrives(slabs.at[n, 0, i], s_r.at[n, 0, i])()
        for k in range(2):
            slab_ring(0, 1, k, 1).start()
            slab_ring(0, 7, k, -1).start()
        hop(ring, 4, 2)
        pass_on(2)
        slab_pass(0)
        hop(slab_ring, 2, 1)
        hop(ring, 4, 3)
        pass_on(3)
        slab_pass(1)
        hop(slab_ring, 2, 2)

        last(ring, 4)
        pass_on(4)
        slab_pass(2)
        apply(0)
        hop(slab_ring, 2, 3)
        slab_pass(3)
        apply(1)
        apply(2)
        last(slab_ring, 2)
        slab_pass(4)
        apply(3)
        apply(4)

        pl.when(y != NY - 1)(move.wait_recv)

        @pl.when(y != NY - 1)
        def _():
            part[n + 1] = acc[...] + shift[n]

        @pl.when(y == NY - 1)
        def _():
            part[n + 1] = acc[...]

        for i in range(8):
            for way in range(4):
                goes, copy = bcast(i, way)
                pl.when(goes)(copy.wait_send)
        for make, pieces in ((ring, 4), (slab_ring, 2)):
            for k in range(pieces):
                for h in range(3):
                    make(h, h + 1, k, 1).wait_send()
                    make((8 - h) % 8, 7 - h, k, -1).wait_send()
                (make(3, 4, k, 1) if 2 * k < pieces else make(5, 4, k, -1)).wait_send()
        for copy in slab_start():
            copy.wait_send()
        for g in range(5):
            for copy in sends(g) + slab_sends(g):
                copy.wait_send()
        pl.when(y != 0)(move.wait_send)
        return carry

    lax.fori_loop(0, STEPS, step, 0)
    for copy in asks():
        copy.wait_send()
    ahead_out[0] = part[STEPS]


def body(incident, pending, self_inverse, retarded, block_rows, block_sources, owner_map):
    p = lax.axis_index("patch")
    x, z = (p // 2) % NX, p // (2 * NX)
    row = block_rows[0, 0]
    source = block_sources[0, 0]
    live = source >= 0
    storage = jnp.sum(jnp.where(source[:, None] == jnp.arange(SRC)[None, :], owner_map[None, :], 0), axis=1)
    owner, local = storage // NB, storage % NB
    d = (z - owner // (2 * NX)) % NZ
    pos = jnp.where(d == 0, 0, jnp.where(d <= 3, 2 * d - 1, jnp.where(d == 4, 7, 2 * (NZ - d))))
    column = ((owner // 2) % NX - x) % NX * 2 + owner % 2
    slot = pos * 8 + column
    code = jnp.arange(LIST, dtype=jnp.int32) * 16 + row * 4 + local
    hit = (slot[None, :] == jnp.arange(64)[:, None]) & live[None, :]
    enc = jnp.max(jnp.where(hit, code[None, :], -1), axis=1).astype(jnp.int32)
    vmem = pl.BlockSpec(memory_space=pltpu.VMEM)
    hbm = pl.BlockSpec(memory_space=pltpu.HBM)
    dma = pltpu.SemaphoreType.DMA
    return pl.pallas_call(
        kernel,
        out_shape=(jax.ShapeDtypeStruct((STEPS, OWN, EXC), jnp.bfloat16),
                   jax.ShapeDtypeStruct((1, OWN, EXC), jnp.float32)),
        in_specs=[pl.BlockSpec(memory_space=pltpu.SMEM), hbm, hbm, hbm, hbm],
        out_specs=(vmem, vmem),
        scratch_shapes=[
            pltpu.VMEM((STEPS, OWN, EXC), jnp.bfloat16),
            pltpu.VMEM((NB, B, B), jnp.float32),
            pltpu.VMEM((LIST, B, B), jnp.float32),
            pltpu.VMEM((NZ, OWN, 8 * B), jnp.bfloat16),
            pltpu.VMEM((STEPS, NZ, NB, B, EXC), jnp.bfloat16),
            pltpu.VMEM((STEPS, NZ, NX - 1, NB, SLAB, EXC), jnp.bfloat16),
            pltpu.VMEM((STEPS, NZ, 8 * B, EXC), jnp.bfloat16),
            pltpu.VMEM((6, NZ, MAIN, EXC), jnp.bfloat16),
            pltpu.VMEM((NZ, B, EXC), jnp.bfloat16),
            pltpu.VMEM((NX - 1, NZ, SLAB, EXC), jnp.bfloat16),
            pltpu.VMEM((STEPS + 1, OWN, EXC), jnp.float32),
            pltpu.VMEM((STEPS, OWN, EXC), jnp.float32),
            pltpu.VMEM((OWN, EXC), jnp.float32),
            pltpu.VMEM((8, NZ * NB, EXC), jnp.float32),
            pltpu.VMEM((8, NZ * NB, EXC), jnp.float32),
            pltpu.VMEM((NX - 1, NZ * NB, EXC), jnp.float32),
            pltpu.VMEM((14, NZ * NB, 16, EXC), jnp.bfloat16),
            dma((4,)), dma((STEPS, 8)), dma((STEPS, NZ, 4)), dma((STEPS, NZ, 3)), dma((STEPS, 5, 8)),
            dma((STEPS, 5, 3)), dma((STEPS,)), dma((11,)),
            dma((4, 8)), dma((NZ, 4)), dma((NZ, 3)), dma((5, 7)), dma((5, 3)), dma, dma((10,)),
        ],
        compiler_params=pltpu.CompilerParams(collective_id=0, has_side_effects=True,
                                             vmem_limit_bytes=48 * 1024 * 1024),
    )(enc, *(pltpu.with_memory_space_constraint(a, pltpu.HBM) for a in (incident, pending, self_inverse, retarded)))


def solution(mesh):
    in_specs = (
        P(None, "patch", None),
        P("lag", "patch", None),
        P("patch", None, None),
        P("lag", "patch", None, None, None),
        P("lag", "patch", None),
        P("lag", "patch", None),
        P(),
    )
    out_specs = (P(None, "patch", None), P("lag", "patch", None))
    return jax.shard_map(body, mesh=mesh, in_specs=in_specs, out_specs=out_specs, check_vma=False)
```

```python
import jax
import jax.numpy as jnp
from jax import lax
from jax.experimental import pallas as pl
from jax.experimental.pallas import tpu as pltpu
from jax.sharding import PartitionSpec as P

EXC = 128
B = 128
NB = 4
OWN = NB * B
STEPS = 4
LIST = 56
SRC = 256
NX, NZ, NY = 4, 8, 8
MESH = pl.DeviceIdType.MESH

ORDER = (0, 1, 7, 2, 6, 3, 5, 4)
GROUPS = ((0, 1), (1, 3), (3, 5), (5, 7), (7, 8))
MAIN, SLAB = 96, 32


def kernel(enc, inc_hbm, pend, sinv_hbm, zmat, cur_out, ahead_out,
           inc, sinv, zf, w, items, slabs, pick, sbuf, pbuf, qbuf, part, shift, acc, want, wanted, wanted2, onehot,
           load_sem, bc_r, z_r, s_r, x_r, p_r, sh_r, q_r,
           bc_s, z_s, s_s, x_s, p_s, sh_s, q_s):
    y = lax.axis_index("lag")
    p = lax.axis_index("patch")
    c = lax.rem(p, 2)
    x = lax.rem(lax.div(p, 2), NX)
    z = lax.div(p, 2 * NX)

    def at(dx=0, dz=0, core=None):
        core = c if core is None else core
        return lax.rem(z + dz + NZ, NZ) * (2 * NX) + lax.rem(x + dx, NX) * 2 + core

    def dev(patch, lag=None):
        return {"lag": y if lag is None else lag, "patch": patch}

    up, down = lax.rem(y + 1, NY), lax.rem(y + NY - 1, NY)
    up2, down2 = lax.rem(y + 2, NY), lax.rem(y + NY - 2, NY)
    partner = 1 - c
    mate = dev(at(core=partner))
    peers = [dev(at(dz=1)), dev(at(dz=-1)), mate, dev(p, up), dev(p, down), dev(p, up2), dev(p, down2)]
    peers += [dev(at(dx=dx, core=k)) for dx in (1, 2, 3) for k in (0, 1)]

    loads = [pltpu.make_async_copy(pend.at[0], part.at[0], load_sem.at[0]),
             pltpu.make_async_copy(inc_hbm, inc, load_sem.at[1]),
             pltpu.make_async_copy(sinv_hbm, sinv, load_sem.at[2]),
             pltpu.make_async_copy(zmat.at[0, 0], zf, load_sem.at[3])]

    barrier = pltpu.get_barrier_semaphore()
    for peer in peers:
        pl.semaphore_signal(barrier, inc=1, device_id=peer, device_id_type=MESH)
    for load in loads:
        load.start()

    def ask(s, carry):
        pos, t = lax.div(s, 8), lax.rem(s, 8)
        local = jnp.maximum(enc[s], 0) & 3
        for k in range(NB):
            want[t, pl.ds(pos * NB + k, 1), :] = jnp.full((1, EXC), jnp.where(local == k, 1.0, 0.0), jnp.float32)
        return carry

    lax.fori_loop(0, 64, ask, 0)
    for load in loads[:3]:
        load.wait()
    pl.semaphore_wait(barrier, len(peers))

    def remote(src, dst, ssem, rsem, where):
        return pltpu.make_async_remote_copy(
            src_ref=src, dst_ref=dst, send_sem=ssem, recv_sem=rsem,
            device_id=where, device_id_type=MESH)

    def arrives(ref, rsem):
        return remote(ref, ref, sh_s, rsem, mate).wait_recv

    def asks():
        out = [remote(want.at[partner], wanted.at[c], q_s.at[0], q_r.at[c], mate)]
        for dx in (1, 2, 3):
            out.append(remote(want.at[dx * 2 + partner], wanted2.at[dx - 1], q_s.at[6 + dx], q_r.at[7 + dx], mate))
            for k in (0, 1):
                t, back = dx * 2 + k, (NX - dx) * 2
                out.append(remote(want.at[t], wanted.at[back + c], q_s.at[t - 1], q_r.at[back + c],
                                  dev(at(dx=dx, core=k))))
        return out

    for copy in asks():
        copy.start()

    def step(n, carry):
        def mine(row):
            return pl.ds(pl.multiple_of(row * B, B), B)

        def piece(i):
            return items.at[n, 0, i // 2, pl.ds((i % 2) * (B // 2), B // 2)]

        def bcast(i, way):
            lag = (up2, down2, up, down)[way]
            goes = ((y == 0) | ((y == 2) & (i < 4)), (y == 0) | ((y == 6) & (i >= 4)),
                    (y == 0) | (y == 2), (y == 0) | (y == 6))[way]
            return goes, remote(piece(i), piece(i), bc_s.at[way, i], bc_r.at[n, i], dev(p, lag))

        def ring(d_from, d_to, k, dz):
            return remote(items.at[n, d_from, k], items.at[n, d_to, k], z_s.at[d_to, k],
                          z_r.at[n, d_to, k], dev(at(dz=dz)))

        def slab_start():
            return [remote(items.at[n, 0, :, pl.ds(MAIN, SLAB)], slabs.at[n, 0, NX - dx - 1], s_s.at[0, dx - 1],
                           s_r.at[n, 0, NX - dx - 1], dev(at(dx=dx))) for dx in (2, 1, 3)]

        def slab_ring(d_from, d_to, k, dz):
            half = pl.ds(2 * k, 2)
            return remote(slabs.at[n, d_from, :, half], slabs.at[n, d_to, :, half], s_s.at[d_to, k],
                          s_r.at[n, d_to, k], dev(at(dz=dz)))

        def span_of(g):
            p0, p1 = GROUPS[g]
            return pl.ds(p0, p1 - p0)

        def sends(g):
            span = span_of(g)
            out = []
            for k in (0, 1):
                out.append(remote(sbuf.at[2 + k, span],
                                  pick.at[n, span, pl.ds(pl.multiple_of((4 + c) * B, B), MAIN)],
                                  x_s.at[g, 3 + k], x_r.at[n, g, 4 + c], dev(at(dx=2, core=k))))
            for dx in (1, 3):
                for k in (0, 1):
                    t, back = dx * 2 + k, (NX - dx) * 2 + c
                    out.append(remote(
                        sbuf.at[t - 2, span], pick.at[n, span, pl.ds(pl.multiple_of(back * B, B), MAIN)],
                        x_s.at[g, t - 1], x_r.at[n, g, back], dev(at(dx=dx, core=k))))
            out.append(remote(pbuf.at[span], pick.at[n, span, mine(c)], x_s.at[g, 0], x_r.at[n, g, c], mate))
            return out

        def slab_sends(g):
            span = span_of(g)
            return [remote(qbuf.at[dx - 1, span],
                           pick.at[n, span, pl.ds(pl.multiple_of((dx * 2 + c) * B + MAIN, SLAB), SLAB)],
                           p_s.at[g, dx - 1], p_r.at[n, g, dx - 1], mate) for dx in (1, 2, 3)]

        def choose(blocks, table, pos, rows):
            total = None
            for k in range(NB):
                term = blocks[k].reshape(rows // 16, 16, EXC) * onehot[table, pos * NB + k][None]
                total = term if total is None else total + term
            return total.reshape(rows, EXC)

        def pass_on(g):
            for pos in range(*GROUPS[g]):
                whole = [items[n, ORDER[pos], k] for k in range(NB)]
                head = [block[:MAIN] for block in whole]
                for t in (4, 5, 2, 3, 6, 7):
                    sbuf[t - 2, pos] = choose(head, t, pos, MAIN)
                pbuf[pos] = choose(whole, partner, pos, B)
                pick[n, pos, mine(c), :] = choose(whole, c, pos, B)
            for copy in sends(g):
                copy.start()

        def slab_pass(g):
            for pos in range(*GROUPS[g]):
                for dx in (1, 2, 3):
                    blocks = [slabs[n, ORDER[pos], dx - 1, k] for k in range(NB)]
                    qbuf[dx - 1, pos] = choose(blocks, 11 + dx - 1, pos, SLAB)
                    rows = pl.ds(pl.multiple_of((dx * 2 + c) * B + MAIN, SLAB), SLAB)
                    pick[n, pos, rows, :] = choose(blocks, 8 + dx - 1, pos, SLAB)
            for copy in slab_sends(g):
                copy.start()

        def apply(g):
            span = span_of(g)
            for s in range(8):
                if s < 2:
                    pl.when(c != s)(arrives(pick.at[n, span, pl.ds(s * B, B)], x_r.at[n, g, s]))
                else:
                    arrives(pick.at[n, span, pl.ds(s * B, MAIN)], x_r.at[n, g, s])()
            for dx in (1, 2, 3):
                rows = pl.ds(pl.multiple_of((dx * 2 + partner) * B + MAIN, SLAB), SLAB)
                arrives(pick.at[n, span, rows], p_r.at[n, g, dx - 1])()
            for pos in range(*GROUPS[g]):
                term = jnp.dot(w[pos], pick[n, pos], preferred_element_type=jnp.float32)
                if pos == 0:
                    acc[...] = term
                else:
                    acc[...] += term

        first = n == 0

        @pl.when(y == 0)
        def _():
            for k in range(NB):
                rows = slice(k * B, (k + 1) * B)
                excess = inc[n, rows].astype(jnp.float32) - part[n, rows]
                solved = jnp.dot(sinv[k], excess, precision=lax.Precision.HIGHEST,
                                 preferred_element_type=jnp.float32)
                items[n, 0, k] = solved.astype(jnp.bfloat16)

        for k in range(NB):
            for i in (2 * k, 2 * k + 1):
                pl.when(y != 0)(arrives(piece(i), bc_r.at[n, i]))
                for way in (0, 1):
                    goes, copy = bcast(i, way)
                    pl.when(goes)(copy.start)
            ring(0, 1, k, 1).start()
            ring(0, 7, k, -1).start()
        for i in range(8):
            for way in (2, 3):
                goes, copy = bcast(i, way)
                pl.when(goes)(copy.start)
        for copy in slab_start():
            copy.start()

        @pl.when(first)
        def _():
            for t in range(8):
                if t < 2:
                    pl.when(c != t)(arrives(wanted.at[t], q_r.at[t]))
                else:
                    arrives(wanted.at[t], q_r.at[t])()
            wanted[c] = want[c]
            for dx in (1, 2, 3):
                arrives(wanted2.at[dx - 1], q_r.at[7 + dx])()

            def line(rows):
                return jnp.broadcast_to(rows, (16, EXC)).astype(jnp.bfloat16)

            def spread(t, carry):
                for r in range(NB * NZ):
                    onehot[t, r] = line(wanted[t, pl.ds(r, 1), :])
                return carry

            def spread_slabs(i, carry):
                for r in range(NB * NZ):
                    onehot[8 + i, r] = line(want[i * 2 + 2 + c, pl.ds(r, 1), :])
                    onehot[11 + i, r] = line(wanted2[i, pl.ds(r, 1), :])
                return carry

            lax.fori_loop(0, 8, spread, 0)
            lax.fori_loop(0, 3, spread_slabs, 0)

        pass_on(0)
        cur_out[n] = items[n, 0].reshape(OWN, EXC)
        move = remote(part.at[n], shift.at[n], sh_s, sh_r.at[n], dev(p, down))
        pl.when(y != 0)(move.start)

        def hop(make, pieces, h):
            for k in range(pieces):
                below = 2 * k < pieces
                make(h - 1, h, k, 1).wait_recv()
                if h < 3 or below:
                    make(h, h + 1, k, 1).start()
                make((9 - h) % 8, 8 - h, k, -1).wait_recv()
                if h < 3 or not below:
                    make(8 - h, 7 - h, k, -1).start()

        def last(make, pieces):
            for k in range(pieces):
                (make(3, 4, k, 1) if 2 * k < pieces else make(5, 4, k, -1)).wait_recv()

        hop(ring, 4, 1)
        pass_on(1)
        for i in range(3):
            arrives(slabs.at[n, 0, i], s_r.at[n, 0, i])()
        for k in range(2):
            slab_ring(0, 1, k, 1).start()
            slab_ring(0, 7, k, -1).start()
        @pl.when(first)
        def _():
            loads[3].wait()

            def place(s, carry):
                code = enc[s]
                row = jnp.where(code < 0, -1, (code >> 2) & 3)
                block = zf[jnp.maximum(code, 0) >> 4].astype(jnp.bfloat16)
                pos, col = lax.div(s, 8), lax.rem(s, 8)
                for r in range(NB):
                    keep = jnp.where(row == r, 1.0, 0.0).astype(jnp.bfloat16)
                    w[pos, pl.ds(r * B, B), pl.ds(pl.multiple_of(col * B, B), B)] = block * keep
                return carry

            lax.fori_loop(0, 64, place, 0)

        hop(ring, 4, 2)
        pass_on(2)
        slab_pass(0)
        hop(slab_ring, 2, 1)
        hop(ring, 4, 3)
        pass_on(3)
        slab_pass(1)
        hop(slab_ring, 2, 2)

        last(ring, 4)
        pass_on(4)
        slab_pass(2)
        apply(0)
        hop(slab_ring, 2, 3)
        slab_pass(3)
        apply(1)
        apply(2)
        last(slab_ring, 2)
        slab_pass(4)
        apply(3)
        apply(4)

        pl.when(y != NY - 1)(move.wait_recv)

        @pl.when(y != NY - 1)
        def _():
            part[n + 1] = acc[...] + shift[n]

        @pl.when(y == NY - 1)
        def _():
            part[n + 1] = acc[...]

        for i in range(8):
            for way in range(4):
                goes, copy = bcast(i, way)
                pl.when(goes)(copy.wait_send)
        for make, pieces in ((ring, 4), (slab_ring, 2)):
            for k in range(pieces):
                for h in range(3):
                    make(h, h + 1, k, 1).wait_send()
                    make((8 - h) % 8, 7 - h, k, -1).wait_send()
                (make(3, 4, k, 1) if 2 * k < pieces else make(5, 4, k, -1)).wait_send()
        for copy in slab_start():
            copy.wait_send()
        for g in range(5):
            for copy in sends(g) + slab_sends(g):
                copy.wait_send()
        pl.when(y != 0)(move.wait_send)
        return carry

    lax.fori_loop(0, STEPS, step, 0)
    for copy in asks():
        copy.wait_send()
    ahead_out[0] = part[STEPS]


def body(incident, pending, self_inverse, retarded, block_rows, block_sources, owner_map):
    p = lax.axis_index("patch")
    x, z = (p // 2) % NX, p // (2 * NX)
    row = block_rows[0, 0]
    source = block_sources[0, 0]
    storage = jnp.max(jnp.where(source[:, None] == jnp.arange(SRC)[None, :], owner_map[None, :], -1), axis=1)
    owner, local = storage // NB, storage % NB
    d = (z - owner // (2 * NX)) % NZ
    pos = jnp.where(d == 0, 0, jnp.where(d <= 3, 2 * d - 1, jnp.where(d == 4, 7, 2 * (NZ - d))))
    column = ((owner // 2) % NX - x) % NX * 2 + owner % 2
    slot = pos * 8 + column
    code = jnp.where(storage < 0, -1, jnp.arange(LIST, dtype=jnp.int32) * 16 + row * 4 + local)
    hit = slot[None, :] == jnp.arange(64)[:, None]
    enc = jnp.max(jnp.where(hit, code[None, :], -1), axis=1).astype(jnp.int32)

    vmem = pl.BlockSpec(memory_space=pltpu.VMEM)
    hbm = pl.BlockSpec(memory_space=pltpu.HBM)
    dma = pltpu.SemaphoreType.DMA
    return pl.pallas_call(
        kernel,
        out_shape=(jax.ShapeDtypeStruct((STEPS, OWN, EXC), jnp.bfloat16),
                   jax.ShapeDtypeStruct((1, OWN, EXC), jnp.float32)),
        in_specs=[pl.BlockSpec(memory_space=pltpu.SMEM), hbm, hbm, hbm, hbm],
        out_specs=(vmem, vmem),
        scratch_shapes=[
            pltpu.VMEM((STEPS, OWN, EXC), jnp.bfloat16),
            pltpu.VMEM((NB, B, B), jnp.float32),
            pltpu.VMEM((LIST, B, B), jnp.float32),
            pltpu.VMEM((NZ, OWN, 8 * B), jnp.bfloat16),
            pltpu.VMEM((STEPS, NZ, NB, B, EXC), jnp.bfloat16),
            pltpu.VMEM((STEPS, NZ, NX - 1, NB, SLAB, EXC), jnp.bfloat16),
            pltpu.VMEM((STEPS, NZ, 8 * B, EXC), jnp.bfloat16),
            pltpu.VMEM((6, NZ, MAIN, EXC), jnp.bfloat16),
            pltpu.VMEM((NZ, B, EXC), jnp.bfloat16),
            pltpu.VMEM((NX - 1, NZ, SLAB, EXC), jnp.bfloat16),
            pltpu.VMEM((STEPS + 1, OWN, EXC), jnp.float32),
            pltpu.VMEM((STEPS, OWN, EXC), jnp.float32),
            pltpu.VMEM((OWN, EXC), jnp.float32),
            pltpu.VMEM((8, NZ * NB, EXC), jnp.float32),
            pltpu.VMEM((8, NZ * NB, EXC), jnp.float32),
            pltpu.VMEM((NX - 1, NZ * NB, EXC), jnp.float32),
            pltpu.VMEM((14, NZ * NB, 16, EXC), jnp.bfloat16),
            dma((4,)), dma((STEPS, 8)), dma((STEPS, NZ, 4)), dma((STEPS, NZ, 3)), dma((STEPS, 5, 8)),
            dma((STEPS, 5, 3)), dma((STEPS,)), dma((11,)),
            dma((4, 8)), dma((NZ, 4)), dma((NZ, 3)), dma((5, 7)), dma((5, 3)), dma, dma((10,)),
        ],
        compiler_params=pltpu.CompilerParams(collective_id=0, has_side_effects=True,
                                             vmem_limit_bytes=48 * 1024 * 1024),
    )(enc, *(pltpu.with_memory_space_constraint(a, pltpu.HBM) for a in (incident, pending, self_inverse, retarded)))


def solution(mesh):
    in_specs = (
        P(None, "patch", None),
        P("lag", "patch", None),
        P("patch", None, None),
        P("lag", "patch", None, None, None),
        P("lag", "patch", None),
        P("lag", "patch", None),
        P(),
    )
    out_specs = (P(None, "patch", None), P("lag", "patch", None))
    return jax.shard_map(body, mesh=mesh, in_specs=in_specs, out_specs=out_specs, check_vma=False)
```

```python
import jax
import jax.numpy as jnp
from jax import lax
from jax.experimental import pallas as pl
from jax.experimental.pallas import tpu as pltpu
from jax.sharding import PartitionSpec as P

EXC = 128
B = 128
NB = 4
OWN = NB * B
STEPS = 4
LIST = 56
SRC = 256
NX, NZ, NY = 4, 8, 8
MESH = pl.DeviceIdType.MESH

ORDER = (0, 1, 7, 2, 6, 3, 5, 4)
GROUPS = ((0, 1), (1, 3), (3, 5), (5, 7), (7, 8))
MAIN, SLAB = 96, 32


def kernel(enc, inc_hbm, pend, sinv_hbm, zmat, cur_out, ahead_out,
           inc, sinv, zf, w, items, slabs, pick, sbuf, pbuf, qbuf, part, shift, acc, want, wanted, wanted2, onehot,
           load_sem, bc_r, z_r, s_r, x_r, p_r, sh_r, q_r,
           bc_s, z_s, s_s, x_s, p_s, sh_s, q_s):
    y = lax.axis_index("lag")
    p = lax.axis_index("patch")
    c = lax.rem(p, 2)
    x = lax.rem(lax.div(p, 2), NX)
    z = lax.div(p, 2 * NX)

    def at(dx=0, dz=0, core=None):
        core = c if core is None else core
        return lax.rem(z + dz + NZ, NZ) * (2 * NX) + lax.rem(x + dx, NX) * 2 + core

    def dev(patch, lag=None):
        return {"lag": y if lag is None else lag, "patch": patch}

    up, down = lax.rem(y + 1, NY), lax.rem(y + NY - 1, NY)
    up2, down2 = lax.rem(y + 2, NY), lax.rem(y + NY - 2, NY)
    partner = 1 - c
    mate = dev(at(core=partner))
    peers = [dev(at(dz=1)), dev(at(dz=-1)), mate, dev(p, up), dev(p, down), dev(p, up2), dev(p, down2)]
    peers += [dev(at(dx=dx, core=k)) for dx in (1, 2, 3) for k in (0, 1)]

    loads = [pltpu.make_async_copy(pend.at[0], part.at[0], load_sem.at[0]),
             pltpu.make_async_copy(inc_hbm, inc, load_sem.at[1]),
             pltpu.make_async_copy(sinv_hbm, sinv, load_sem.at[2]),
             pltpu.make_async_copy(zmat.at[0, 0], zf, load_sem.at[3])]

    barrier = pltpu.get_barrier_semaphore()
    for peer in peers:
        pl.semaphore_signal(barrier, inc=1, device_id=peer, device_id_type=MESH)
    for load in loads:
        load.start()

    def ask(s, carry):
        pos, t = lax.div(s, 8), lax.rem(s, 8)
        local = jnp.maximum(enc[s], 0) & 3
        for k in range(NB):
            want[t, pl.ds(pos * NB + k, 1), :] = jnp.full((1, EXC), jnp.where(local == k, 1.0, 0.0), jnp.float32)
        return carry

    lax.fori_loop(0, 64, ask, 0)

    def line(rows):
        return jnp.broadcast_to(rows, (16, EXC)).astype(jnp.bfloat16)

    def spread_own(i, carry):
        for r in range(NB * NZ):
            onehot[8 + i, r] = line(want[i * 2 + 2 + c, pl.ds(r, 1), :])
        return carry

    lax.fori_loop(0, 3, spread_own, 0)
    for load in loads[:3]:
        load.wait()
    pl.semaphore_wait(barrier, len(peers))

    def remote(src, dst, ssem, rsem, where):
        return pltpu.make_async_remote_copy(
            src_ref=src, dst_ref=dst, send_sem=ssem, recv_sem=rsem,
            device_id=where, device_id_type=MESH)

    def arrives(ref, rsem):
        return remote(ref, ref, sh_s, rsem, mate).wait_recv

    def asks():
        out = [remote(want.at[partner], wanted.at[c], q_s.at[0], q_r.at[c], mate)]
        for dx in (1, 2, 3):
            out.append(remote(want.at[dx * 2 + partner], wanted2.at[dx - 1], q_s.at[6 + dx], q_r.at[7 + dx], mate))
            for k in (0, 1):
                t, back = dx * 2 + k, (NX - dx) * 2
                out.append(remote(want.at[t], wanted.at[back + c], q_s.at[t - 1], q_r.at[back + c],
                                  dev(at(dx=dx, core=k))))
        return out

    for copy in asks():
        copy.start()

    def step(n, carry):
        def mine(row):
            return pl.ds(pl.multiple_of(row * B, B), B)

        def piece(i):
            return items.at[n, 0, i // 2, pl.ds((i % 2) * (B // 2), B // 2)]

        def bcast(i, way):
            lag = (up2, down2, up, down)[way]
            goes = ((y == 0) | ((y == 2) & (i < 4)), (y == 0) | ((y == 6) & (i >= 4)),
                    (y == 0) | (y == 2), (y == 0) | (y == 6))[way]
            return goes, remote(piece(i), piece(i), bc_s.at[way, i], bc_r.at[n, i], dev(p, lag))

        def ring(d_from, d_to, k, dz):
            return remote(items.at[n, d_from, k], items.at[n, d_to, k], z_s.at[d_to, k],
                          z_r.at[n, d_to, k], dev(at(dz=dz)))

        def slab_start():
            return [remote(items.at[n, 0, :, pl.ds(MAIN, SLAB)], slabs.at[n, 0, NX - dx - 1], s_s.at[0, dx - 1],
                           s_r.at[n, 0, NX - dx - 1], dev(at(dx=dx))) for dx in (2, 1, 3)]

        def slab_ring(d_from, d_to, k, dz):
            half = pl.ds(2 * k, 2)
            return remote(slabs.at[n, d_from, :, half], slabs.at[n, d_to, :, half], s_s.at[d_to, k],
                          s_r.at[n, d_to, k], dev(at(dz=dz)))

        def span_of(g):
            p0, p1 = GROUPS[g]
            return pl.ds(p0, p1 - p0)

        def sends(g):
            span = span_of(g)
            out = []
            for k in (0, 1):
                out.append(remote(sbuf.at[2 + k, span],
                                  pick.at[n, span, pl.ds(pl.multiple_of((4 + c) * B, B), MAIN)],
                                  x_s.at[g, 3 + k], x_r.at[n, g, 4 + c], dev(at(dx=2, core=k))))
            for dx in (1, 3):
                for k in (0, 1):
                    t, back = dx * 2 + k, (NX - dx) * 2 + c
                    out.append(remote(
                        sbuf.at[t - 2, span], pick.at[n, span, pl.ds(pl.multiple_of(back * B, B), MAIN)],
                        x_s.at[g, t - 1], x_r.at[n, g, back], dev(at(dx=dx, core=k))))
            out.append(remote(pbuf.at[span], pick.at[n, span, mine(c)], x_s.at[g, 0], x_r.at[n, g, c], mate))
            return out

        def slab_sends(g):
            span = span_of(g)
            return [remote(qbuf.at[dx - 1, span],
                           pick.at[n, span, pl.ds(pl.multiple_of((dx * 2 + c) * B + MAIN, SLAB), SLAB)],
                           p_s.at[g, dx - 1], p_r.at[n, g, dx - 1], mate) for dx in (1, 2, 3)]

        def choose(blocks, table, pos, rows):
            total = None
            for k in range(NB):
                term = blocks[k].reshape(rows // 16, 16, EXC) * onehot[table, pos * NB + k][None]
                total = term if total is None else total + term
            return total.reshape(rows, EXC)

        def pass_on(g):
            for pos in range(*GROUPS[g]):
                whole = [items[n, ORDER[pos], k] for k in range(NB)]
                head = [block[:MAIN] for block in whole]
                for t in (4, 5, 2, 3, 6, 7):
                    sbuf[t - 2, pos] = choose(head, t, pos, MAIN)
                pbuf[pos] = choose(whole, partner, pos, B)
                pick[n, pos, mine(c), :] = choose(whole, c, pos, B)
            for copy in sends(g):
                copy.start()

        def slab_pass(g):
            for pos in range(*GROUPS[g]):
                for dx in (1, 2, 3):
                    blocks = [slabs[n, ORDER[pos], dx - 1, k] for k in range(NB)]
                    qbuf[dx - 1, pos] = choose(blocks, 11 + dx - 1, pos, SLAB)
                    rows = pl.ds(pl.multiple_of((dx * 2 + c) * B + MAIN, SLAB), SLAB)
                    pick[n, pos, rows, :] = choose(blocks, 8 + dx - 1, pos, SLAB)
            for copy in slab_sends(g):
                copy.start()

        def apply(g):
            span = span_of(g)
            for s in range(8):
                if s < 2:
                    pl.when(c != s)(arrives(pick.at[n, span, pl.ds(s * B, B)], x_r.at[n, g, s]))
                else:
                    arrives(pick.at[n, span, pl.ds(s * B, MAIN)], x_r.at[n, g, s])()
            for dx in (1, 2, 3):
                rows = pl.ds(pl.multiple_of((dx * 2 + partner) * B + MAIN, SLAB), SLAB)
                arrives(pick.at[n, span, rows], p_r.at[n, g, dx - 1])()
            for pos in range(*GROUPS[g]):
                term = jnp.dot(w[pos], pick[n, pos], preferred_element_type=jnp.float32)
                if pos == 0:
                    acc[...] = term
                else:
                    acc[...] += term

        first = n == 0

        @pl.when(y == 0)
        def _():
            for k in range(NB):
                rows = slice(k * B, (k + 1) * B)
                excess = inc[n, rows].astype(jnp.float32) - part[n, rows]
                solved = jnp.dot(sinv[k], excess, precision=lax.Precision.HIGHEST,
                                 preferred_element_type=jnp.float32)
                items[n, 0, k] = solved.astype(jnp.bfloat16)

        for k in range(NB):
            for i in (2 * k, 2 * k + 1):
                pl.when(y != 0)(arrives(piece(i), bc_r.at[n, i]))
                for way in (0, 1):
                    goes, copy = bcast(i, way)
                    pl.when(goes)(copy.start)
            ring(0, 1, k, 1).start()
            ring(0, 7, k, -1).start()
        for i in range(8):
            for way in (2, 3):
                goes, copy = bcast(i, way)
                pl.when(goes)(copy.start)
        for copy in slab_start():
            copy.start()

        @pl.when(first)
        def _():
            for t in range(8):
                if t < 2:
                    pl.when(c != t)(arrives(wanted.at[t], q_r.at[t]))
                else:
                    arrives(wanted.at[t], q_r.at[t])()
            wanted[c] = want[c]
            for dx in (1, 2, 3):
                arrives(wanted2.at[dx - 1], q_r.at[7 + dx])()

            def spread(t, carry):
                for r in range(NB * NZ):
                    onehot[t, r] = line(wanted[t, pl.ds(r, 1), :])
                return carry

            def spread_slabs(i, carry):
                for r in range(NB * NZ):
                    onehot[11 + i, r] = line(wanted2[i, pl.ds(r, 1), :])
                return carry

            lax.fori_loop(0, 8, spread, 0)
            lax.fori_loop(0, 3, spread_slabs, 0)

        pass_on(0)
        cur_out[n] = items[n, 0].reshape(OWN, EXC)
        move = remote(part.at[n], shift.at[n], sh_s, sh_r.at[n], dev(p, down))
        pl.when(y != 0)(move.start)

        def hop(make, pieces, h):
            for k in range(pieces):
                below = 2 * k < pieces
                make(h - 1, h, k, 1).wait_recv()
                if h < 3 or below:
                    make(h, h + 1, k, 1).start()
                make((9 - h) % 8, 8 - h, k, -1).wait_recv()
                if h < 3 or not below:
                    make(8 - h, 7 - h, k, -1).start()

        def last(make, pieces):
            for k in range(pieces):
                (make(3, 4, k, 1) if 2 * k < pieces else make(5, 4, k, -1)).wait_recv()

        hop(ring, 4, 1)
        pass_on(1)
        for i in range(3):
            arrives(slabs.at[n, 0, i], s_r.at[n, 0, i])()
        for k in range(2):
            slab_ring(0, 1, k, 1).start()
            slab_ring(0, 7, k, -1).start()
        @pl.when(first)
        def _():
            loads[3].wait()

            def place(s, carry):
                code = enc[s]
                row = jnp.where(code < 0, -1, (code >> 2) & 3)
                block = zf[jnp.maximum(code, 0) >> 4].astype(jnp.bfloat16)
                pos, col = lax.div(s, 8), lax.rem(s, 8)
                for r in range(NB):
                    keep = jnp.where(row == r, 1.0, 0.0).astype(jnp.bfloat16)
                    w[pos, pl.ds(r * B, B), pl.ds(pl.multiple_of(col * B, B), B)] = block * keep
                return carry

            lax.fori_loop(0, 64, place, 0)

        hop(ring, 4, 2)
        pass_on(2)
        slab_pass(0)
        hop(slab_ring, 2, 1)
        hop(ring, 4, 3)
        pass_on(3)
        slab_pass(1)
        hop(slab_ring, 2, 2)

        last(ring, 4)
        pass_on(4)
        slab_pass(2)
        apply(0)
        hop(slab_ring, 2, 3)
        slab_pass(3)
        apply(1)
        apply(2)
        last(slab_ring, 2)
        slab_pass(4)
        apply(3)
        apply(4)

        pl.when(y != NY - 1)(move.wait_recv)

        @pl.when(y != NY - 1)
        def _():
            part[n + 1] = acc[...] + shift[n]

        @pl.when(y == NY - 1)
        def _():
            part[n + 1] = acc[...]

        for i in range(8):
            for way in range(4):
                goes, copy = bcast(i, way)
                pl.when(goes)(copy.wait_send)
        for make, pieces in ((ring, 4), (slab_ring, 2)):
            for k in range(pieces):
                for h in range(3):
                    make(h, h + 1, k, 1).wait_send()
                    make((8 - h) % 8, 7 - h, k, -1).wait_send()
                (make(3, 4, k, 1) if 2 * k < pieces else make(5, 4, k, -1)).wait_send()
        for copy in slab_start():
            copy.wait_send()
        for g in range(5):
            for copy in sends(g) + slab_sends(g):
                copy.wait_send()
        pl.when(y != 0)(move.wait_send)
        return carry

    lax.fori_loop(0, STEPS, step, 0)
    for copy in asks():
        copy.wait_send()
    ahead_out[0] = part[STEPS]


def body(incident, pending, self_inverse, retarded, block_rows, block_sources, owner_map):
    p = lax.axis_index("patch")
    x, z = (p // 2) % NX, p // (2 * NX)
    row = block_rows[0, 0]
    source = block_sources[0, 0]
    storage = jnp.max(jnp.where(source[:, None] == jnp.arange(SRC)[None, :], owner_map[None, :], -1), axis=1)
    owner, local = storage // NB, storage % NB
    d = (z - owner // (2 * NX)) % NZ
    pos = jnp.where(d == 0, 0, jnp.where(d <= 3, 2 * d - 1, jnp.where(d == 4, 7, 2 * (NZ - d))))
    column = ((owner // 2) % NX - x) % NX * 2 + owner % 2
    slot = pos * 8 + column
    code = jnp.where(storage < 0, -1, jnp.arange(LIST, dtype=jnp.int32) * 16 + row * 4 + local)
    hit = slot[None, :] == jnp.arange(64)[:, None]
    enc = jnp.max(jnp.where(hit, code[None, :], -1), axis=1).astype(jnp.int32)

    vmem = pl.BlockSpec(memory_space=pltpu.VMEM)
    hbm = pl.BlockSpec(memory_space=pltpu.HBM)
    dma = pltpu.SemaphoreType.DMA
    return pl.pallas_call(
        kernel,
        out_shape=(jax.ShapeDtypeStruct((STEPS, OWN, EXC), jnp.bfloat16),
                   jax.ShapeDtypeStruct((1, OWN, EXC), jnp.float32)),
        in_specs=[pl.BlockSpec(memory_space=pltpu.SMEM), hbm, hbm, hbm, hbm],
        out_specs=(vmem, vmem),
        scratch_shapes=[
            pltpu.VMEM((STEPS, OWN, EXC), jnp.bfloat16),
            pltpu.VMEM((NB, B, B), jnp.float32),
            pltpu.VMEM((LIST, B, B), jnp.float32),
            pltpu.VMEM((NZ, OWN, 8 * B), jnp.bfloat16),
            pltpu.VMEM((STEPS, NZ, NB, B, EXC), jnp.bfloat16),
            pltpu.VMEM((STEPS, NZ, NX - 1, NB, SLAB, EXC), jnp.bfloat16),
            pltpu.VMEM((STEPS, NZ, 8 * B, EXC), jnp.bfloat16),
            pltpu.VMEM((6, NZ, MAIN, EXC), jnp.bfloat16),
            pltpu.VMEM((NZ, B, EXC), jnp.bfloat16),
            pltpu.VMEM((NX - 1, NZ, SLAB, EXC), jnp.bfloat16),
            pltpu.VMEM((STEPS + 1, OWN, EXC), jnp.float32),
            pltpu.VMEM((STEPS, OWN, EXC), jnp.float32),
            pltpu.VMEM((OWN, EXC), jnp.float32),
            pltpu.VMEM((8, NZ * NB, EXC), jnp.float32),
            pltpu.VMEM((8, NZ * NB, EXC), jnp.float32),
            pltpu.VMEM((NX - 1, NZ * NB, EXC), jnp.float32),
            pltpu.VMEM((14, NZ * NB, 16, EXC), jnp.bfloat16),
            dma((4,)), dma((STEPS, 8)), dma((STEPS, NZ, 4)), dma((STEPS, NZ, 3)), dma((STEPS, 5, 8)),
            dma((STEPS, 5, 3)), dma((STEPS,)), dma((11,)),
            dma((4, 8)), dma((NZ, 4)), dma((NZ, 3)), dma((5, 7)), dma((5, 3)), dma, dma((10,)),
        ],
        compiler_params=pltpu.CompilerParams(collective_id=0, has_side_effects=True,
                                             vmem_limit_bytes=48 * 1024 * 1024),
    )(enc, *(pltpu.with_memory_space_constraint(a, pltpu.HBM) for a in (incident, pending, self_inverse, retarded)))


def solution(mesh):
    in_specs = (
        P(None, "patch", None),
        P("lag", "patch", None),
        P("patch", None, None),
        P("lag", "patch", None, None, None),
        P("lag", "patch", None),
        P("lag", "patch", None),
        P(),
    )
    out_specs = (P(None, "patch", None), P("lag", "patch", None))
    return jax.shard_map(body, mesh=mesh, in_specs=in_specs, out_specs=out_specs, check_vma=False)
```
